256 devices in a mesh: wheel: 32 (over x_hi, z, core), slab: 8 (over x_lo, y).
Axes of the slice: x: 4 (x_hi: 2, x_lo: 2; x = x_hi * 2 + x_lo), y: 4, z: 8, core: 2. Of those that a mesh axis runs over, the one named last changes fastest.
Arguments:
- krylov_block: float32 [2, 64, 3, 16, 2048], P(None, 'wheel', None, None, 'slab'), may hold values from -6 to 6
- blade_class: int32 [64], P('wheel'), may hold values from 0 to 3
- neighbors: int32 [8, 2048], P(None, 'slab'), may hold values from 0 to 511
- iface_rows: int32 [2, 512], P(None, 'slab'), may hold values from 0 to 255
- face_rows: int32 [2, 512], P(None, 'slab'), may hold values from 0 to 255
- stiffness: float32 [3, 3, 8, 2048], P(None, None, None, 'slab'), may hold values from -1.25 to 1.25
- lumped_mass: float32 [3, 2048], P(None, 'slab'), may hold values from 0.5 to 2
- precond: bfloat16 [32, 64, 384, 384], P('wheel', 'slab'), may hold values from -0.3125 to 0.3125
Outputs:
- preconditioned: float32 [32, 64, 16, 384], P('wheel', 'slab')
The draws below stay inside these ranges and needn't reach their ends.
Inputs may be any that keep to these rules, and one draw needn't show every extreme that they name: `neighbors`: extended numbering: own nodes first (256), then 64 from the lower slab, 64 from the upper slab, 64 from the previous sector, 64 from the next sector.
All inputs are finite; a program needn't handle non-finite values.
Results may differ from the reference program's by a relative error of at most 0.0039.
Values may be sent and summed in bfloat16 or wider, within the bound.
A program may use at most 64 MiB of HBM per device.

```python
import math
import jax
import jax.numpy as jnp
from jax import lax

NODES_DEV = 256
VECS = 16
NB = 8
IFACE = 64
CYC = 64
GROUP = 32
SECTORS = 64
PAIRS = 32
NODES = 2048
GROUPS = 64
BLOCK = 384
N_SLAB = 8


def set_ends(drawn, key, smallest, high):
    extent = drawn.shape
    spot = [jax.random.randint(jax.random.fold_in(key, axis), (), 0, extent[axis]) for axis in range(len(extent))]
    drawn = drawn.at[tuple(spot)].set(smallest)
    longest = extent.index(max(extent))
    spot[longest] = (spot[longest] + 1) % extent[longest]
    return drawn.at[tuple(spot)].set(high)


def level_of(rng, extent, cuts, least, high):
    factor_of = 1.0
    for position, parts in cuts:
        steps = jax.random.uniform(jax.random.fold_in(jax.random.fold_in(rng, 6), position), (parts,), jnp.float32, least / len(cuts), high / len(cuts))
        factor_of = factor_of * jnp.repeat(jnp.exp(steps), extent[position] // parts).reshape((-1,) + (1,) * (len(extent) - 1 - position))
    return factor_of


def scatter_about(key, extent, width, most, split=(), held_as=jnp.bfloat16):
    level = level_of(key, extent, split, -0.22, 0.18) if split else 1.0
    drawn = jax.random.normal(key, extent, jnp.float32) * width * level
    return jnp.minimum(jnp.maximum(drawn, -most), most).astype(held_as)


def setup_inputs(seed: int = 0) -> dict:
    seeds = jax.random.split(jax.random.key(seed), 9)
    return {
        "krylov_block": scatter_about(seeds[0], (2, SECTORS, 3, VECS, NODES), 1.0, 6.0, ((1, 32), (4, 8)), jnp.float32),
        "blade_class": set_ends(jax.random.randint(seeds[1], (SECTORS,), 0, 4), jax.random.fold_in(seeds[1], 1), 0, 3).astype(jnp.int32),
        "neighbors": set_ends(jax.random.randint(seeds[2], (NB, NODES), 0, NODES_DEV + 2 * IFACE + 2 * CYC), jax.random.fold_in(seeds[2], 1), 0, (NODES_DEV + 2 * IFACE + 2 * CYC) - 1).astype(jnp.int32),
        "iface_rows": set_ends(jax.random.randint(seeds[3], (2, IFACE * N_SLAB), 0, NODES_DEV), jax.random.fold_in(seeds[3], 1), 0, NODES_DEV - 1).astype(jnp.int32),
        "face_rows": set_ends(jax.random.randint(seeds[4], (2, CYC * N_SLAB), 0, NODES_DEV), jax.random.fold_in(seeds[4], 1), 0, NODES_DEV - 1).astype(jnp.int32),
        "stiffness": scatter_about(seeds[5], (3, 3, NB, NODES), (3 * NB) ** -0.5, 1.25, ((3, 8),), jnp.float32),
        "lumped_mass": jnp.clip(jnp.exp(math.log(2.0) - 1.3862944 * jax.random.uniform(seeds[6], (3, NODES), jnp.float32) ** level_of(seeds[6], (3, NODES), ((1, 8),), -0.2, 0.2)), 0.5, 2.0),
        "precond": scatter_about(seeds[7], (PAIRS, GROUPS, BLOCK, BLOCK), BLOCK ** -0.5, 0.3125, ((0, 32), (1, 8))),
    }


damping_ratio = 0.5
gyro_rate = 0.8
shift_value = 0.3
class_step = 0.125

def basis(row_ids, col_ids, sectors_all):
    pair_id = row_ids[:, None] // 2
    part_id = row_ids[:, None] % 2
    sector_id = col_ids[None, :]
    phases = pair_id * sector_id % sectors_all
    angles = 2.0 * math.pi / sectors_all * phases.astype(jnp.float32)
    parity = (1 - 2 * (sector_id % 2)).astype(jnp.float32)
    edge_rows = jnp.where(part_id == 0, jnp.ones_like(angles), parity * jnp.ones_like(angles)) * math.sqrt(1.0 / sectors_all)
    inner_rows = jnp.where(part_id == 0, jnp.cos(angles), jnp.sin(angles)) * math.sqrt(2.0 / sectors_all)
    return jnp.where(pair_id == 0, edge_rows, inner_rows).astype(jnp.float32)

def arrange(harmonic):
    pair_rows, states, comps, vectors, nodes = harmonic.shape
    shaped = harmonic.reshape(pair_rows // 2, 2, states, comps, vectors, nodes // GROUP, GROUP)
    shaped = shaped.transpose(0, 5, 4, 1, 2, 3, 6)
    return shaped.reshape(pair_rows // 2, nodes // GROUP, vectors, 4 * comps * GROUP)

def reference(krylov_block, blade_class, neighbors, iface_rows, face_rows, stiffness, lumped_mass, precond):
    displacement = krylov_block[0]
    velocity = krylov_block[1]
    moved_field = displacement + damping_ratio * velocity
    rim_width = iface_rows.shape[1] // N_SLAB
    face_width = face_rows.shape[1] // N_SLAB
    pieces = []
    for slab_index in range(N_SLAB):
        first_node = slab_index * NODES_DEV
        own_nodes = moved_field[..., first_node:first_node + NODES_DEV]
        if slab_index > 0:
            below_nodes = moved_field[..., first_node - NODES_DEV:first_node]
            from_lower = jnp.take(below_nodes, iface_rows[1, (slab_index - 1) * rim_width:slab_index * rim_width], axis=3)
        else:
            from_lower = jnp.zeros(own_nodes.shape[:3] + (rim_width,), jnp.float32)
        if slab_index < N_SLAB - 1:
            above_nodes = moved_field[..., first_node + NODES_DEV:first_node + 2 * NODES_DEV]
            from_upper = jnp.take(above_nodes, iface_rows[0, (slab_index + 1) * rim_width:(slab_index + 2) * rim_width], axis=3)
        else:
            from_upper = jnp.zeros(own_nodes.shape[:3] + (rim_width,), jnp.float32)
        left_face = jnp.take(own_nodes, face_rows[0, slab_index * face_width:(slab_index + 1) * face_width], axis=3)
        right_face = jnp.take(own_nodes, face_rows[1, slab_index * face_width:(slab_index + 1) * face_width], axis=3)
        from_prev = jnp.roll(right_face, 1, axis=0)
        from_next = jnp.roll(left_face, -1, axis=0)
        extended = jnp.concatenate((own_nodes, from_lower, from_upper, from_prev, from_next), axis=3)
        picked = jnp.take(extended, neighbors[:, first_node:first_node + NODES_DEV], axis=3)
        pieces.append(jnp.einsum('cdkn,sdvkn->scvn', stiffness[..., first_node:first_node + NODES_DEV], picked, precision=lax.Precision.HIGHEST))
    restore = jnp.concatenate(pieces, axis=3)
    scale = (1.0 + class_step * blade_class.astype(jnp.float32))[:, None, None, None]
    gyro = gyro_rate * jnp.stack((-lumped_mass[0] * velocity[:, 1], lumped_mass[1] * velocity[:, 0], jnp.zeros_like(velocity[:, 2])), axis=1)
    res_disp = velocity - shift_value * displacement
    res_velo = -scale * restore - gyro - shift_value * lumped_mass[None, :, None, :] * velocity
    residual = jnp.stack((res_disp, res_velo), axis=0)
    sectors_all = residual.shape[1]
    table = basis(jnp.arange(sectors_all, dtype=jnp.int32), jnp.arange(sectors_all, dtype=jnp.int32), sectors_all)
    harmonic = jnp.einsum('bs,tscvn->btcvn', table, residual, precision=lax.Precision.HIGHEST).astype(jnp.bfloat16)
    lhs = arrange(harmonic)
    return jnp.einsum('pgvj,pgij->pgvi', lhs.astype(jnp.float32), precond.astype(jnp.float32))
```

```python
import math

import jax
import jax.numpy as jnp
import numpy as np
from jax import lax
from jax.experimental import pallas as pl
from jax.experimental.pallas import tpu as pltpu
from jax.sharding import PartitionSpec as P

import ml_dtypes

damping_ratio = 0.5
gyro_rate = 0.8
shift_value = 0.3
class_step = 0.125

SECT = 64
WHEEL = 32
SLAB = 8
MESH = pl.DeviceIdType.MESH
BF = jnp.bfloat16
F32 = jnp.float32


def basis_table():
    b = np.arange(SECT)[:, None]
    s = np.arange(SECT)[None, :]
    p, q = b // 2, b % 2
    angle = 2.0 * math.pi / SECT * ((p * s) % SECT)
    inner = np.where(q == 0, np.cos(angle), np.sin(angle)) * math.sqrt(2.0 / SECT)
    edge = np.where(q == 0, 1.0, 1.0 - 2.0 * (s % 2)) * math.sqrt(1.0 / SECT)
    return np.where(p == 0, edge, inner).astype(np.float32)


def kron_table():
    full = np.kron(basis_table(), np.eye(8, dtype=np.float32))
    high = full.astype(ml_dtypes.bfloat16)
    low = (full - high.astype(np.float32)).astype(ml_dtypes.bfloat16)
    return np.stack((high, low))


def one_hot(rows, cols, index_row):
    at = lax.broadcasted_iota(jnp.int32, (rows, cols), 0)
    return jnp.where(at == index_row, 1.0, 0.0).astype(BF)


def kernel(
    kb, bc, nb, ifr, fcr, st, ms, pc_hbm, km_hbm, out,
    pcv, kmv, hs, hsw, hr, hrw, sb, rv1, sb2, rv2,
    lsem, hsend, hrecv, ssem1, rsem1, ssem2, rsem2,
):
    w = lax.axis_index("wheel")
    j = lax.axis_index("slab")

    barrier = pltpu.get_barrier_semaphore()

    @pl.loop(1, WHEEL)
    def _(i):
        pl.semaphore_signal(
            barrier, inc=1, device_id={"wheel": lax.rem(w + i, WHEEL)}, device_id_type=MESH
        )

    up = lax.rem(j + 1, SLAB)
    down = lax.rem(j + SLAB - 1, SLAB)
    nxt = lax.rem(w + 1, WHEEL)
    prv = lax.rem(w + WHEEL - 1, WHEEL)
    for slab in (up, down):
        pl.semaphore_signal(barrier, inc=1, device_id={"slab": slab}, device_id_type=MESH)

    copy_km = pltpu.make_async_copy(km_hbm, kmv, lsem.at[0])
    copy_pc = pltpu.make_async_copy(pc_hbm, pcv, lsem.at[1])
    copy_km.start()
    copy_pc.start()

    u = kb[0]
    v = kb[1]
    e = (u + damping_ratio * v).reshape(96, 256)
    ehi = e.astype(BF)
    elo = (e - ehi.astype(F32)).astype(BF)

    none = jnp.full((1, 64), -1, jnp.int32)
    index = jnp.concatenate(
        (ifr[1:2, :], none, none, ifr[0:1, :], fcr[1:2, :], none, none, fcr[0:1, :]), axis=1
    )
    picks = jnp.dot(ehi, one_hot(256, 512, index), preferred_element_type=F32)
    hs[0] = picks[:, 0:128].astype(BF)
    hs[1] = picks[:, 128:256].astype(BF)
    hsw[0] = picks[48:96, 256:384].astype(BF)
    hsw[1] = picks[0:48, 384:512].astype(BF)

    pl.semaphore_wait(barrier, WHEEL + 1)

    halos = [
        pltpu.make_async_remote_copy(
            src_ref=src, dst_ref=dst, send_sem=hsend.at[n], recv_sem=hrecv.at[n],
            device_id=to, device_id_type=MESH,
        )
        for n, (src, dst, to) in enumerate(
            (
                (hs.at[0], hr.at[0], {"slab": up}),
                (hs.at[1], hr.at[1], {"slab": down}),
                (hsw.at[0], hrw.at[0], {"wheel": nxt}),
                (hsw.at[1], hrw.at[1], {"wheel": prv}),
            )
        )
    ]
    for copy in halos:
        copy.start()

    lane = lax.broadcasted_iota(jnp.int32, (32, 128), 1)
    spot = lane // 32

    def pack(t, res):
        for h in range(2):
            part = [res[:, c, :, h * 128 : (h + 1) * 128].reshape(32, 128) for c in range(3)]
            one = pltpu.roll(part[1], 32, 1)
            two = pltpu.roll(part[2], 64, 1)
            for g in range(4):
                tile = jnp.where(
                    spot == (g + 1) % 4, one, jnp.where(spot == (g + 2) % 4, two, part[0])
                )
                for half in range(2):
                    rows = jnp.concatenate(
                        (tile[half * 8 : half * 8 + 8], tile[16 + half * 8 : 24 + half * 8]), axis=0
                    )
                    sb[t, (h * 4 + g) * 2 + half] = rows.astype(BF)

    def send(t):
        @pl.loop(0, 16)
        def _(i):
            gv = lax.rem(w // 2 + i, 16)
            to = gv * 2 + t

            @pl.when(to != w)
            def _():
                pltpu.make_async_remote_copy(
                    src_ref=sb.at[t, gv], dst_ref=rv1.at[w], send_sem=ssem1, recv_sem=rsem1,
                    device_id={"wheel": to}, device_id_type=MESH,
                ).start()

    pack(0, v - shift_value * u)
    send(0)

    def stencil(ke, k, picked):
        picked = picked.reshape(2, 3, 16, 256)
        for c in range(3):
            for d in range(3):
                ke[c] = ke[c] + st[c, d, k : k + 1, :] * picked[:, d]
        return ke

    own = jnp.concatenate((ehi, elo), axis=0)
    ke = [jnp.zeros((2, 16, 256), F32) for _ in range(3)]
    for k in range(8):
        both = jnp.dot(own, one_hot(256, 256, nb[k : k + 1, :]), preferred_element_type=F32)
        ke = stencil(ke, k, both[:96] + both[96:])

    for copy in halos:
        copy.wait()
    zero = jnp.zeros((96, 128), F32)
    iface = jnp.where(j > 0, hr[0].astype(F32), zero) + jnp.where(j < SLAB - 1, hr[1].astype(F32), zero)
    face = jnp.concatenate(
        (
            hrw[0].astype(F32) + picks[48:96, 384:512],
            hrw[1].astype(F32) + picks[0:48, 256:384],
        ),
        axis=0,
    )
    halo = jnp.concatenate((iface, face), axis=1).astype(BF)
    for k in range(8):
        ke = stencil(
            ke, k, jnp.dot(halo, one_hot(256, 256, nb[k : k + 1, :] - 256), preferred_element_type=F32)
        )

    mass = [ms[c : c + 1, :] for c in range(3)]
    gyro = (-(mass[0] * v[:, 1]), mass[1] * v[:, 0], None)
    rows = []
    for c in range(3):
        scaled = jnp.stack(
            [(1.0 + class_step * bc[s].astype(F32)) * ke[c][s] for s in range(2)], axis=0
        )
        row = -scaled - shift_value * (mass[c] * v[:, c])
        if c < 2:
            row = row - gyro_rate * gyro[c]
        rows.append(row)
    pack(1, jnp.stack(rows, axis=1))
    send(1)

    rv1[w] = sb[lax.rem(w, 2), w // 2]
    pltpu.make_async_copy(rv1.at[pl.ds(0, WHEEL - 1)], rv1.at[pl.ds(0, WHEEL - 1)], rsem1).wait()
    copy_km.wait()
    field = rv1[...].reshape(512, 128)
    har = jnp.dot(kmv[0], field, preferred_element_type=F32) + jnp.dot(
        kmv[1], field, preferred_element_type=F32
    )
    sb2[...] = har.astype(BF).reshape(32, 16, 128)

    @pl.loop(1, WHEEL)
    def _(i):
        to = lax.rem(w + i, WHEEL)
        pltpu.make_async_remote_copy(
            src_ref=sb2.at[to], dst_ref=rv2.at[w], send_sem=ssem2, recv_sem=rsem2,
            device_id={"wheel": to}, device_id_type=MESH,
        ).start()

    rv2[w] = sb2[w]
    pltpu.make_async_copy(rv2.at[pl.ds(0, WHEEL - 1)], rv2.at[pl.ds(0, WHEEL - 1)], rsem2).wait()
    copy_pc.wait()
    lane16 = lax.broadcasted_iota(jnp.int32, (16, 128), 1)
    for g in range(8):
        turned = []
        for q in range(2):
            for t in range(2):
                x = jnp.concatenate(
                    [
                        rv2[(g * 2 + half) * 2 + t].astype(F32)[q * 8 : q * 8 + 8]
                        for half in range(2)
                    ],
                    axis=0,
                )
                shift = (96 * (2 * q + t) - 32 * (g % 4)) % 128
                turned.append(pltpu.roll(x, shift, 1) if shift else x)
        lhs = jnp.concatenate(
            (
                jnp.where(lane16 < 96, turned[0], turned[1]),
                jnp.where(lane16 < 64, turned[1], turned[2]),
                jnp.where(lane16 < 32, turned[2], turned[3]),
            ),
            axis=1,
        ).astype(BF)
        out[0, g] = lax.dot_general(
            lhs, pcv[0, g], (((1,), (1,)), ((), ())), preferred_element_type=F32
        )

    pltpu.make_async_copy(rv1.at[pl.ds(0, WHEEL - 1)], rv1.at[pl.ds(0, WHEEL - 1)], ssem1).wait()
    pltpu.make_async_copy(rv2.at[pl.ds(0, WHEEL - 1)], rv2.at[pl.ds(0, WHEEL - 1)], ssem2).wait()


def on_device(
    krylov_block, blade_class, neighbors, iface_rows, face_rows, stiffness, lumped_mass, precond
):
    vmem = pl.BlockSpec(memory_space=pltpu.VMEM)
    hbm = pl.BlockSpec(memory_space=pl.ANY)
    return pl.pallas_call(
        kernel,
        out_shape=jax.ShapeDtypeStruct((1, 8, 16, 384), F32),
        in_specs=[vmem, pl.BlockSpec(memory_space=pltpu.SMEM)] + [vmem] * 5 + [hbm, hbm],
        out_specs=vmem,
        scratch_shapes=[
            pltpu.VMEM((1, 8, 384, 384), BF),
            pltpu.VMEM((2, 512, 512), BF),
            pltpu.VMEM((2, 96, 128), BF),
            pltpu.VMEM((2, 48, 128), BF),
            pltpu.VMEM((2, 96, 128), BF),
            pltpu.VMEM((2, 48, 128), BF),
            pltpu.VMEM((2, 16, 16, 128), BF),
            pltpu.VMEM((32, 16, 128), BF),
            pltpu.VMEM((32, 16, 128), BF),
            pltpu.VMEM((32, 16, 128), BF),
            pltpu.SemaphoreType.DMA((2,)),
            pltpu.SemaphoreType.DMA((4,)),
            pltpu.SemaphoreType.DMA((4,)),
            pltpu.SemaphoreType.DMA,
            pltpu.SemaphoreType.DMA,
            pltpu.SemaphoreType.DMA,
            pltpu.SemaphoreType.DMA,
        ],
        compiler_params=pltpu.CompilerParams(
            collective_id=0, has_side_effects=True, vmem_limit_bytes=40 * 1024 * 1024
        ),
    )(
        krylov_block, blade_class, neighbors, iface_rows, face_rows, stiffness, lumped_mass,
        precond, jnp.asarray(kron_table()),
    )


def solution(mesh):
    return jax.shard_map(
        on_device,
        mesh=mesh,
        in_specs=(
            P(None, "wheel", None, None, "slab"),
            P("wheel"),
            P(None, "slab"),
            P(None, "slab"),
            P(None, "slab"),
            P(None, None, None, "slab"),
            P(None, "slab"),
            P("wheel", "slab", None, None),
        ),
        out_specs=P("wheel", "slab", None, None),
        check_vma=False,
    )
```

```python
import math

import jax
import jax.numpy as jnp
import numpy as np
from jax import lax
from jax.experimental import pallas as pl
from jax.experimental.pallas import tpu as pltpu
from jax.sharding import PartitionSpec as P

import ml_dtypes

damping_ratio = 0.5
gyro_rate = 0.8
shift_value = 0.3
class_step = 0.125

SECT = 64
WHEEL = 32
SLAB = 8
MESH = pl.DeviceIdType.MESH
BF = jnp.bfloat16
F32 = jnp.float32


def basis_table():
    b = np.arange(SECT)[:, None]
    s = np.arange(SECT)[None, :]
    p, q = b // 2, b % 2
    angle = 2.0 * math.pi / SECT * ((p * s) % SECT)
    inner = np.where(q == 0, np.cos(angle), np.sin(angle)) * math.sqrt(2.0 / SECT)
    edge = np.where(q == 0, 1.0, 1.0 - 2.0 * (s % 2)) * math.sqrt(1.0 / SECT)
    return np.where(p == 0, edge, inner).astype(np.float32)


def kron_table():
    full = np.kron(basis_table(), np.eye(8, dtype=np.float32))
    high = full.astype(ml_dtypes.bfloat16)
    low = (full - high.astype(np.float32)).astype(ml_dtypes.bfloat16)
    return np.stack((high, low))


def one_hot(rows, cols, index_row):
    at = lax.broadcasted_iota(jnp.int32, (rows, cols), 0)
    return jnp.where(at == index_row, 1.0, 0.0).astype(BF)


def kernel(
    kb_hbm, bc_hbm, nb_hbm, ifr_hbm, fcr_hbm, st_hbm, ms_hbm, pc_hbm, km_hbm, out,
    kb, bc, nb, ifr, fcr, st, ms, pcv, kmv, hs, hsw, hr, hrw, sb, rv1, sb2, rv2,
    lsem, hsend, hrecv, ssem1, rsem1, ssem2, rsem2,
):
    w = lax.axis_index("wheel")
    j = lax.axis_index("slab")

    loads = [
        pltpu.make_async_copy(src, dst, lsem.at[n])
        for n, (src, dst) in enumerate(
            (
                (kb_hbm, kb), (ifr_hbm, ifr), (fcr_hbm, fcr), (nb_hbm, nb), (st_hbm, st),
                (ms_hbm, ms), (bc_hbm, bc), (km_hbm, kmv), (pc_hbm, pcv),
            )
        )
    ]
    for load in loads:
        load.start()

    barrier = pltpu.get_barrier_semaphore()

    @pl.loop(1, WHEEL)
    def _(i):
        pl.semaphore_signal(
            barrier, inc=1, device_id={"wheel": lax.rem(w + i, WHEEL)}, device_id_type=MESH
        )

    up = lax.rem(j + 1, SLAB)
    down = lax.rem(j + SLAB - 1, SLAB)
    nxt = lax.rem(w + 1, WHEEL)
    prv = lax.rem(w + WHEEL - 1, WHEEL)
    for slab in (up, down):
        pl.semaphore_signal(barrier, inc=1, device_id={"slab": slab}, device_id_type=MESH)

    for load in loads[:3]:
        load.wait()
    u = kb[0]
    v = kb[1]
    e = (u + damping_ratio * v).reshape(96, 256)
    ehi = e.astype(BF)
    elo = (e - ehi.astype(F32)).astype(BF)

    none = jnp.full((1, 64), -1, jnp.int32)
    index = jnp.concatenate(
        (ifr[1:2, :], none, none, ifr[0:1, :], fcr[1:2, :], none, none, fcr[0:1, :]), axis=1
    )
    picks = jnp.dot(ehi, one_hot(256, 512, index), preferred_element_type=F32)
    hs[0] = picks[:, 0:128].astype(BF)
    hs[1] = picks[:, 128:256].astype(BF)
    hsw[0] = picks[48:96, 256:384].astype(BF)
    hsw[1] = picks[0:48, 384:512].astype(BF)

    pl.semaphore_wait(barrier, WHEEL + 1)

    halos = [
        pltpu.make_async_remote_copy(
            src_ref=src, dst_ref=dst, send_sem=hsend.at[n], recv_sem=hrecv.at[n],
            device_id=to, device_id_type=MESH,
        )
        for n, (src, dst, to) in enumerate(
            (
                (hs.at[0], hr.at[0], {"slab": up}),
                (hs.at[1], hr.at[1], {"slab": down}),
                (hsw.at[0], hrw.at[0], {"wheel": nxt}),
                (hsw.at[1], hrw.at[1], {"wheel": prv}),
            )
        )
    ]
    for copy in halos:
        copy.start()

    lane = lax.broadcasted_iota(jnp.int32, (32, 128), 1)
    spot = lane // 32

    def pack(t, res):
        for h in range(2):
            part = [res[:, c, :, h * 128 : (h + 1) * 128].reshape(32, 128) for c in range(3)]
            one = pltpu.roll(part[1], 32, 1)
            two = pltpu.roll(part[2], 64, 1)
            for g in range(4):
                tile = jnp.where(
                    spot == (g + 1) % 4, one, jnp.where(spot == (g + 2) % 4, two, part[0])
                )
                for half in range(2):
                    rows = jnp.concatenate(
                        (tile[half * 8 : half * 8 + 8], tile[16 + half * 8 : 24 + half * 8]), axis=0
                    )
                    sb[t, (h * 4 + g) * 2 + half] = rows.astype(BF)

    def send(t):
        @pl.loop(0, 16)
        def _(i):
            gv = lax.rem(w // 2 + i, 16)
            to = gv * 2 + t

            @pl.when(to != w)
            def _():
                pltpu.make_async_remote_copy(
                    src_ref=sb.at[t, gv], dst_ref=rv1.at[w], send_sem=ssem1, recv_sem=rsem1,
                    device_id={"wheel": to}, device_id_type=MESH,
                ).start()

    pack(0, v - shift_value * u)
    send(0)

    def stencil(ke, k, picked):
        picked = picked.reshape(2, 3, 16, 256)
        for c in range(3):
            for d in range(3):
                ke[c] = ke[c] + st[c, d, k : k + 1, :] * picked[:, d]
        return ke

    for load in loads[3:7]:
        load.wait()
    own = jnp.concatenate((ehi, elo), axis=0)
    ke = [jnp.zeros((2, 16, 256), F32) for _ in range(3)]
    for k in range(8):
        both = jnp.dot(own, one_hot(256, 256, nb[k : k + 1, :]), preferred_element_type=F32)
        ke = stencil(ke, k, both[:96] + both[96:])

    for copy in halos:
        copy.wait()
    zero = jnp.zeros((96, 128), F32)
    iface = jnp.where(j > 0, hr[0].astype(F32), zero) + jnp.where(j < SLAB - 1, hr[1].astype(F32), zero)
    face = jnp.concatenate(
        (
            hrw[0].astype(F32) + picks[48:96, 384:512],
            hrw[1].astype(F32) + picks[0:48, 256:384],
        ),
        axis=0,
    )
    halo = jnp.concatenate((iface, face), axis=1).astype(BF)
    for k in range(8):
        ke = stencil(
            ke, k, jnp.dot(halo, one_hot(256, 256, nb[k : k + 1, :] - 256), preferred_element_type=F32)
        )

    mass = [ms[c : c + 1, :] for c in range(3)]
    gyro = (-(mass[0] * v[:, 1]), mass[1] * v[:, 0], None)
    rows = []
    for c in range(3):
        scaled = jnp.stack(
            [(1.0 + class_step * bc[s].astype(F32)) * ke[c][s] for s in range(2)], axis=0
        )
        row = -scaled - shift_value * (mass[c] * v[:, c])
        if c < 2:
            row = row - gyro_rate * gyro[c]
        rows.append(row)
    pack(1, jnp.stack(rows, axis=1))
    send(1)

    rv1[w] = sb[lax.rem(w, 2), w // 2]
    pltpu.make_async_copy(rv1.at[pl.ds(0, WHEEL - 1)], rv1.at[pl.ds(0, WHEEL - 1)], rsem1).wait()
    loads[7].wait()
    field = rv1[...].reshape(512, 128)
    har = jnp.dot(kmv[0], field, preferred_element_type=F32) + jnp.dot(
        kmv[1], field, preferred_element_type=F32
    )
    sb2[...] = har.astype(BF).reshape(32, 16, 128)

    @pl.loop(1, WHEEL)
    def _(i):
        to = lax.rem(w + i, WHEEL)
        pltpu.make_async_remote_copy(
            src_ref=sb2.at[to], dst_ref=rv2.at[w], send_sem=ssem2, recv_sem=rsem2,
            device_id={"wheel": to}, device_id_type=MESH,
        ).start()

    rv2[w] = sb2[w]
    pltpu.make_async_copy(rv2.at[pl.ds(0, WHEEL - 1)], rv2.at[pl.ds(0, WHEEL - 1)], rsem2).wait()
    loads[8].wait()
    lane16 = lax.broadcasted_iota(jnp.int32, (16, 128), 1)
    for g in range(8):
        turned = []
        for q in range(2):
            for t in range(2):
                x = jnp.concatenate(
                    [
                        rv2[(g * 2 + half) * 2 + t].astype(F32)[q * 8 : q * 8 + 8]
                        for half in range(2)
                    ],
                    axis=0,
                )
                shift = (96 * (2 * q + t) - 32 * (g % 4)) % 128
                turned.append(pltpu.roll(x, shift, 1) if shift else x)
        lhs = jnp.concatenate(
            (
                jnp.where(lane16 < 96, turned[0], turned[1]),
                jnp.where(lane16 < 64, turned[1], turned[2]),
                jnp.where(lane16 < 32, turned[2], turned[3]),
            ),
            axis=1,
        ).astype(BF)
        out[0, g] = lax.dot_general(
            lhs, pcv[0, g], (((1,), (1,)), ((), ())), preferred_element_type=F32
        )

    pltpu.make_async_copy(rv1.at[pl.ds(0, WHEEL - 1)], rv1.at[pl.ds(0, WHEEL - 1)], ssem1).wait()
    pltpu.make_async_copy(rv2.at[pl.ds(0, WHEEL - 1)], rv2.at[pl.ds(0, WHEEL - 1)], ssem2).wait()


def on_device(
    krylov_block, blade_class, neighbors, iface_rows, face_rows, stiffness, lumped_mass, precond
):
    vmem = pl.BlockSpec(memory_space=pltpu.VMEM)
    hbm = pl.BlockSpec(memory_space=pltpu.HBM)
    return pl.pallas_call(
        kernel,
        out_shape=jax.ShapeDtypeStruct((1, 8, 16, 384), F32),
        in_specs=[hbm] * 9,
        out_specs=vmem,
        scratch_shapes=[
            pltpu.VMEM((2, 2, 3, 16, 256), F32),
            pltpu.SMEM((2,), jnp.int32),
            pltpu.VMEM((8, 256), jnp.int32),
            pltpu.VMEM((2, 64), jnp.int32),
            pltpu.VMEM((2, 64), jnp.int32),
            pltpu.VMEM((3, 3, 8, 256), F32),
            pltpu.VMEM((3, 256), F32),
            pltpu.VMEM((1, 8, 384, 384), BF),
            pltpu.VMEM((2, 512, 512), BF),
            pltpu.VMEM((2, 96, 128), BF),
            pltpu.VMEM((2, 48, 128), BF),
            pltpu.VMEM((2, 96, 128), BF),
            pltpu.VMEM((2, 48, 128), BF),
            pltpu.VMEM((2, 16, 16, 128), BF),
            pltpu.VMEM((32, 16, 128), BF),
            pltpu.VMEM((32, 16, 128), BF),
            pltpu.VMEM((32, 16, 128), BF),
            pltpu.SemaphoreType.DMA((9,)),
            pltpu.SemaphoreType.DMA((4,)),
            pltpu.SemaphoreType.DMA((4,)),
            pltpu.SemaphoreType.DMA,
            pltpu.SemaphoreType.DMA,
            pltpu.SemaphoreType.DMA,
            pltpu.SemaphoreType.DMA,
        ],
        compiler_params=pltpu.CompilerParams(
            collective_id=0, has_side_effects=True, vmem_limit_bytes=60 * 1024 * 1024
        ),
    )(
        krylov_block, blade_class, neighbors, iface_rows, face_rows, stiffness, lumped_mass,
        precond, jnp.asarray(kron_table()),
    )


def solution(mesh):
    return jax.shard_map(
        on_device,
        mesh=mesh,
        in_specs=(
            P(None, "wheel", None, None, "slab"),
            P("wheel"),
            P(None, "slab"),
            P(None, "slab"),
            P(None, "slab"),
            P(None, None, None, "slab"),
            P(None, "slab"),
            P("wheel", "slab", None, None),
        ),
        out_specs=P("wheel", "slab", None, None),
        check_vma=False,
    )
```

```python
import math

import jax
import jax.numpy as jnp
import numpy as np
from jax import lax
from jax.experimental import pallas as pl
from jax.experimental.pallas import tpu as pltpu
from jax.sharding import PartitionSpec as P

import ml_dtypes

damping_ratio = 0.5
gyro_rate = 0.8
shift_value = 0.3
class_step = 0.125

SECT = 64
WHEEL = 32
SLAB = 8
MESH = pl.DeviceIdType.MESH
BF = jnp.bfloat16
F32 = jnp.float32


def slot_of(w):
    return (w // 8 % 2) * 16 + (w // 16) * 8 + w % 8


def worker_of(t, g):
    return (12 + g) % 16 if t else 16 + g


def basis_table():
    b = np.arange(SECT)[:, None]
    s = np.arange(SECT)[None, :]
    p, q = b // 2, b % 2
    angle = 2.0 * math.pi / SECT * ((p * s) % SECT)
    inner = np.where(q == 0, np.cos(angle), np.sin(angle)) * math.sqrt(2.0 / SECT)
    edge = np.where(q == 0, 1.0, 1.0 - 2.0 * (s % 2)) * math.sqrt(1.0 / SECT)
    return np.where(p == 0, edge, inner).astype(np.float32)


def kron_table():
    sectors = [2 * w + part for w in sorted(range(WHEEL), key=slot_of) for part in range(2)]
    full = np.kron(basis_table()[:, sectors], np.eye(8, dtype=np.float32))
    high = full.astype(ml_dtypes.bfloat16)
    low = (full - high.astype(np.float32)).astype(ml_dtypes.bfloat16)
    return np.stack((high, low))


def one_hot(rows, cols, index_row):
    at = lax.broadcasted_iota(jnp.int32, (rows, cols), 0)
    return jnp.where(at == index_row, 1.0, 0.0).astype(BF)


def kernel(
    kb_hbm, bc_hbm, nb_hbm, ifr_hbm, fcr_hbm, st_hbm, ms_hbm, pc_hbm, km_hbm, out,
    kb, bc, nb, ifr, fcr, st, ms, pcv, kmv, hs, hsw, hr, hrw, sb, rv1, acc, sb2, rv2,
    lsem, hsend, hrecv, ssem1, rsem1, ssem2, rsem2,
):
    w = lax.axis_index("wheel")
    j = lax.axis_index("slab")

    loads = [
        pltpu.make_async_copy(src, dst, lsem.at[n])
        for n, (src, dst) in enumerate(
            (
                (kb_hbm, kb), (ifr_hbm, ifr), (fcr_hbm, fcr), (nb_hbm, nb), (st_hbm, st),
                (ms_hbm, ms), (bc_hbm, bc), (km_hbm, kmv), (pc_hbm, pcv),
            )
        )
    ]
    for load in loads:
        load.start()

    barrier = pltpu.get_barrier_semaphore()

    up = lax.rem(j + 1, SLAB)
    down = lax.rem(j + SLAB - 1, SLAB)
    nxt = lax.rem(w + 1, WHEEL)
    prv = lax.rem(w + WHEEL - 1, WHEEL)
    for to in ({"wheel": nxt}, {"wheel": prv}, {"slab": up}, {"slab": down}):
        pl.semaphore_signal(barrier, inc=1, device_id=to, device_id_type=MESH)

    my_t = jnp.where(w < 16, 1, 0)
    my_g = jnp.where(w < 16, lax.rem(w + 4, 16), w - 16)
    works = my_g < 8

    @pl.when(works)
    def _():
        @pl.loop(1, WHEEL)
        def _(i):
            pl.semaphore_signal(
                barrier, inc=1, device_id={"wheel": lax.rem(w + i, WHEEL)}, device_id_type=MESH
            )

    for load in loads[:3]:
        load.wait()
    u = kb[0]
    v = kb[1]
    e = (u + damping_ratio * v).reshape(96, 256)
    ehi = e.astype(BF)
    elo = (e - ehi.astype(F32)).astype(BF)

    none = jnp.full((1, 64), -1, jnp.int32)
    index = jnp.concatenate(
        (ifr[1:2, :], none, none, ifr[0:1, :], fcr[1:2, :], none, none, fcr[0:1, :]), axis=1
    )
    picks = jnp.dot(ehi, one_hot(256, 512, index), preferred_element_type=F32)
    hs[0] = picks[:, 0:128].astype(BF)
    hs[1] = picks[:, 128:256].astype(BF)
    hsw[0] = picks[48:96, 256:384].astype(BF)
    hsw[1] = picks[0:48, 384:512].astype(BF)

    pl.semaphore_wait(barrier, jnp.where(works, 19, 20))

    halos = [
        pltpu.make_async_remote_copy(
            src_ref=src, dst_ref=dst, send_sem=hsend.at[n], recv_sem=hrecv.at[n],
            device_id=to, device_id_type=MESH,
        )
        for n, (src, dst, to) in enumerate(
            (
                (hs.at[0], hr.at[0], {"slab": up}),
                (hs.at[1], hr.at[1], {"slab": down}),
                (hsw.at[0], hrw.at[0], {"wheel": nxt}),
                (hsw.at[1], hrw.at[1], {"wheel": prv}),
            )
        )
    ]
    for copy in halos:
        copy.start()

    lane = lax.broadcasted_iota(jnp.int32, (32, 128), 1)
    spot = lane // 32

    def pack(t, res):
        for h in range(2):
            part = [res[:, c, :, h * 128 : (h + 1) * 128].reshape(32, 128) for c in range(3)]
            one = pltpu.roll(part[1], 32, 1)
            two = pltpu.roll(part[2], 64, 1)
            for g in range(4):
                tile = jnp.where(
                    spot == (g + 1) % 4, one, jnp.where(spot == (g + 2) % 4, two, part[0])
                )
                for half in range(2):
                    rows = jnp.concatenate(
                        (tile[half * 8 : half * 8 + 8], tile[16 + half * 8 : 24 + half * 8]), axis=0
                    )
                    sb[t, h * 4 + g, half] = rows.astype(BF)

    slot = lax.rem(w // 8, 2) * 16 + (w // 16) * 8 + lax.rem(w, 8)
    half_sem = rsem1.at[lax.rem(w // 8, 2)]

    def send(t):
        for g in range(8):
            to = worker_of(t, g)

            @pl.when(w != to)
            def _():
                pltpu.make_async_remote_copy(
                    src_ref=sb.at[t, g], dst_ref=rv1.at[slot], send_sem=ssem1, recv_sem=half_sem,
                    device_id={"wheel": to}, device_id_type=MESH,
                ).start()

            @pl.when(w == to)
            def _():
                pltpu.make_async_copy(sb.at[t, g], rv1.at[slot], half_sem).start()

    pack(0, v - shift_value * u)
    send(0)

    def stencil(ke, k, picked):
        picked = picked.reshape(2, 3, 16, 256)
        for c in range(3):
            for d in range(3):
                ke[c] = ke[c] + st[c, d, k : k + 1, :] * picked[:, d]
        return ke

    for load in loads[3:7]:
        load.wait()
    own = jnp.concatenate((ehi, elo), axis=0)
    ke = [jnp.zeros((2, 16, 256), F32) for _ in range(3)]
    for k in range(8):
        both = jnp.dot(own, one_hot(256, 256, nb[k : k + 1, :]), preferred_element_type=F32)
        ke = stencil(ke, k, both[:96] + both[96:])

    for copy in halos:
        copy.wait()
    zero = jnp.zeros((96, 128), F32)
    iface = jnp.where(j > 0, hr[0].astype(F32), zero) + jnp.where(j < SLAB - 1, hr[1].astype(F32), zero)
    face = jnp.concatenate(
        (
            hrw[0].astype(F32) + picks[48:96, 384:512],
            hrw[1].astype(F32) + picks[0:48, 256:384],
        ),
        axis=0,
    )
    halo = jnp.concatenate((iface, face), axis=1).astype(BF)
    for k in range(8):
        ke = stencil(
            ke, k, jnp.dot(halo, one_hot(256, 256, nb[k : k + 1, :] - 256), preferred_element_type=F32)
        )

    mass = [ms[c : c + 1, :] for c in range(3)]
    gyro = (-(mass[0] * v[:, 1]), mass[1] * v[:, 0], None)
    rows = []
    for c in range(3):
        scaled = jnp.stack(
            [(1.0 + class_step * bc[s].astype(F32)) * ke[c][s] for s in range(2)], axis=0
        )
        row = -scaled - shift_value * (mass[c] * v[:, c])
        if c < 2:
            row = row - gyro_rate * gyro[c]
        rows.append(row)
    pack(1, jnp.stack(rows, axis=1))
    send(1)

    @pl.when(works)
    def _():
        loads[7].wait()

        def field(part):
            both = rv1[part * 16 : part * 16 + 16]
            return jnp.concatenate(
                (both[:, 0].reshape(256, 128), both[:, 1].reshape(256, 128)), axis=1
            )

        def transform(first, part, data):
            rows = slice(first * 256, first * 256 + 256)
            cols = slice(part * 256, part * 256 + 256)
            return jnp.dot(kmv[0, rows, cols], data, preferred_element_type=F32) + jnp.dot(
                kmv[1, rows, cols], data, preferred_element_type=F32
            )

        def arrived(part):
            whole = rv1.at[pl.ds(part * 16, 16)]
            pltpu.make_async_copy(whole, whole, rsem1.at[part]).wait()

        arrived(0)
        near = field(0)
        for first in range(2):
            acc[first] = transform(first, 0, near)
        arrived(1)
        far = field(1)
        for first in range(2):
            har = (acc[first] + transform(first, 1, far)).reshape(16, 2, 8, 256)
            sb2[first * 16 : first * 16 + 16] = jnp.concatenate(
                (har[..., :128], har[..., 128:]), axis=2
            ).astype(BF)
            for z in (0, 1, 2, 3, 7, 6, 5, 4):
                for core in range(2):
                    to = first * 16 + z * 2 + core

                    @pl.when(w != to)
                    def _():
                        pltpu.make_async_remote_copy(
                            src_ref=sb2.at[to], dst_ref=rv2.at[my_t, my_g], send_sem=ssem2,
                            recv_sem=rsem2.at[my_t], device_id={"wheel": to}, device_id_type=MESH,
                        ).start()

                    @pl.when(w == to)
                    def _():
                        pltpu.make_async_copy(
                            sb2.at[to], rv2.at[my_t, my_g], rsem2.at[my_t]
                        ).start()

    for t in range(2):
        pltpu.make_async_copy(rv2.at[t], rv2.at[t], rsem2.at[t]).wait()
    loads[8].wait()
    lane16 = lax.broadcasted_iota(jnp.int32, (16, 128), 1)
    for g in range(8):
        turned = []
        for q in range(2):
            for t in range(2):
                x = rv2[t, g, q].astype(F32)
                shift = (96 * (2 * q + t) - 32 * (g % 4)) % 128
                turned.append(pltpu.roll(x, shift, 1) if shift else x)
        lhs = jnp.concatenate(
            (
                jnp.where(lane16 < 96, turned[0], turned[1]),
                jnp.where(lane16 < 64, turned[1], turned[2]),
                jnp.where(lane16 < 32, turned[2], turned[3]),
            ),
            axis=1,
        ).astype(BF)
        out[0, g] = lax.dot_general(
            lhs, pcv[0, g], (((1,), (1,)), ((), ())), preferred_element_type=F32
        )

    def sent(count, sem):
        whole = rv1.at[pl.ds(0, count)]
        pltpu.make_async_copy(whole, whole, sem).wait()

    @pl.when(works)
    def _():
        sent(15, ssem1)
        sent(31, ssem2)

    @pl.when(jnp.logical_not(works))
    def _():
        loads[7].wait()
        sent(16, ssem1)


def on_device(
    krylov_block, blade_class, neighbors, iface_rows, face_rows, stiffness, lumped_mass, precond
):
    vmem = pl.BlockSpec(memory_space=pltpu.VMEM)
    hbm = pl.BlockSpec(memory_space=pltpu.HBM)
    return pl.pallas_call(
        kernel,
        out_shape=jax.ShapeDtypeStruct((1, 8, 16, 384), F32),
        in_specs=[hbm] * 9,
        out_specs=vmem,
        scratch_shapes=[
            pltpu.VMEM((2, 2, 3, 16, 256), F32),
            pltpu.SMEM((2,), jnp.int32),
            pltpu.VMEM((8, 256), jnp.int32),
            pltpu.VMEM((2, 64), jnp.int32),
            pltpu.VMEM((2, 64), jnp.int32),
            pltpu.VMEM((3, 3, 8, 256), F32),
            pltpu.VMEM((3, 256), F32),
            pltpu.VMEM((1, 8, 384, 384), BF),
            pltpu.VMEM((2, 512, 512), BF),
            pltpu.VMEM((2, 96, 128), BF),
            pltpu.VMEM((2, 48, 128), BF),
            pltpu.VMEM((2, 96, 128), BF),
            pltpu.VMEM((2, 48, 128), BF),
            pltpu.VMEM((2, 8, 2, 16, 128), BF),
            pltpu.VMEM((32, 2, 16, 128), BF),
            pltpu.VMEM((2, 256, 256), F32),
            pltpu.VMEM((32, 2, 16, 128), BF),
            pltpu.VMEM((2, 8, 2, 16, 128), BF),
            pltpu.SemaphoreType.DMA((9,)),
            pltpu.SemaphoreType.DMA((4,)),
            pltpu.SemaphoreType.DMA((4,)),
            pltpu.SemaphoreType.DMA,
            pltpu.SemaphoreType.DMA((2,)),
            pltpu.SemaphoreType.DMA,
            pltpu.SemaphoreType.DMA((2,)),
        ],
        compiler_params=pltpu.CompilerParams(
            collective_id=0, has_side_effects=True, vmem_limit_bytes=60 * 1024 * 1024
        ),
    )(
        krylov_block, blade_class, neighbors, iface_rows, face_rows, stiffness, lumped_mass,
        precond, jnp.asarray(kron_table()),
    )


def solution(mesh):
    return jax.shard_map(
        on_device,
        mesh=mesh,
        in_specs=(
            P(None, "wheel", None, None, "slab"),
            P("wheel"),
            P(None, "slab"),
            P(None, "slab"),
            P(None, "slab"),
            P(None, None, None, "slab"),
            P(None, "slab"),
            P("wheel", "slab", None, None),
        ),
        out_specs=P("wheel", "slab", None, None),
        check_vma=False,
    )
```

```python
import math

import jax
import jax.numpy as jnp
import numpy as np
from jax import lax
from jax.experimental import pallas as pl
from jax.experimental.pallas import tpu as pltpu
from jax.sharding import PartitionSpec as P

import ml_dtypes

damping_ratio = 0.5
gyro_rate = 0.8
shift_value = 0.3
class_step = 0.125

SECT = 64
WHEEL = 32
SLAB = 8
MESH = pl.DeviceIdType.MESH
BF = jnp.bfloat16
F32 = jnp.float32


def slot_of(w):
    return (w // 8 % 2) * 16 + (w // 16) * 8 + w % 8


def worker_of(t, g):
    return (g // 4) * 16 + ((7 + g % 4) % 8) * 2 + t


def basis_table():
    b = np.arange(SECT)[:, None]
    s = np.arange(SECT)[None, :]
    p, q = b // 2, b % 2
    angle = 2.0 * math.pi / SECT * ((p * s) % SECT)
    inner = np.where(q == 0, np.cos(angle), np.sin(angle)) * math.sqrt(2.0 / SECT)
    edge = np.where(q == 0, 1.0, 1.0 - 2.0 * (s % 2)) * math.sqrt(1.0 / SECT)
    return np.where(p == 0, edge, inner).astype(np.float32)


def kron_table():
    sectors = [2 * w + part for w in sorted(range(WHEEL), key=slot_of) for part in range(2)]
    full = np.kron(basis_table()[:, sectors], np.eye(8, dtype=np.float32))
    high = full.astype(ml_dtypes.bfloat16)
    low = (full - high.astype(np.float32)).astype(ml_dtypes.bfloat16)
    return np.stack((high, low))


def one_hot(rows, cols, index_row):
    at = lax.broadcasted_iota(jnp.int32, (rows, cols), 0)
    return jnp.where(at == index_row, 1.0, 0.0).astype(BF)


def kernel(
    kb_hbm, bc_hbm, nb_hbm, ifr_hbm, fcr_hbm, st_hbm, ms_hbm, pc_hbm, km_hbm, out,
    kb, bc, nb, ifr, fcr, st, ms, pcv, kmv, hs, hsw, hr, hrw, sb, rv1, acc, sb2, rv2,
    lsem, hsend, hrecv, ssem1, rsem1, ssem2, rsem2,
):
    w = lax.axis_index("wheel")
    j = lax.axis_index("slab")

    up = lax.rem(j + 1, SLAB)
    down = lax.rem(j + SLAB - 1, SLAB)
    nxt = lax.rem(w + 1, WHEEL)
    prv = lax.rem(w + WHEEL - 1, WHEEL)
    loads = [
        pltpu.make_async_copy(src, dst, lsem.at[n])
        for n, (src, dst) in enumerate(
            (
                (kb_hbm, kb), (ifr_hbm, ifr), (fcr_hbm, fcr), (nb_hbm, nb), (st_hbm, st),
                (ms_hbm, ms), (bc_hbm, bc), (km_hbm, kmv), (pc_hbm, pcv),
            )
        )
    ]
    for load in loads:
        load.start()

    barrier = pltpu.get_barrier_semaphore()
    has_up = j < SLAB - 1
    has_down = j > 0

    def greet(to):
        pl.semaphore_signal(barrier, inc=1, device_id=to, device_id_type=MESH)

    @pl.when(has_up)
    def _():
        greet({"slab": up})

    @pl.when(has_down)
    def _():
        greet({"slab": down})

    greet({"wheel": nxt})
    greet({"wheel": prv})

    my_t = lax.rem(w, 2)
    along = lax.rem(lax.rem(w // 2, 8) + 1, 8)
    my_g = (w // 16) * 4 + along
    works = along < 4

    @pl.when(works)
    def _():
        @pl.loop(1, WHEEL)
        def _(i):
            greet({"wheel": lax.rem(w + i, WHEEL)})

    for load in loads[:3]:
        load.wait()
    u = kb[0]
    v = kb[1]
    e = (u + damping_ratio * v).reshape(96, 256)
    ehi = e.astype(BF)
    elo = (e - ehi.astype(F32)).astype(BF)

    none = jnp.full((1, 64), -1, jnp.int32)
    index = jnp.concatenate(
        (ifr[1:2, :], none, none, ifr[0:1, :], fcr[1:2, :], none, none, fcr[0:1, :]), axis=1
    )
    picks = jnp.dot(ehi, one_hot(256, 512, index), preferred_element_type=F32)
    hs[0] = picks[:, 0:128].astype(BF)
    hs[1] = picks[:, 128:256].astype(BF)
    hsw[0] = picks[48:96, 256:384].astype(BF)
    hsw[1] = picks[0:48, 384:512].astype(BF)

    pl.semaphore_wait(
        barrier,
        18 + jnp.where(has_up, 1, 0) + jnp.where(has_down, 1, 0) - jnp.where(works, 1, 0),
    )

    halos = [
        pltpu.make_async_remote_copy(
            src_ref=src, dst_ref=dst, send_sem=hsend.at[n], recv_sem=hrecv.at[n],
            device_id=to, device_id_type=MESH,
        )
        for n, (src, dst, to) in enumerate(
            (
                (hs.at[0], hr.at[0], {"slab": up}),
                (hs.at[1], hr.at[1], {"slab": down}),
                (hsw.at[0], hrw.at[0], {"wheel": nxt}),
                (hsw.at[1], hrw.at[1], {"wheel": prv}),
            )
        )
    ]

    @pl.when(has_up)
    def _():
        halos[0].start()

    @pl.when(has_down)
    def _():
        halos[1].start()

    halos[2].start()
    halos[3].start()

    lane = lax.broadcasted_iota(jnp.int32, (32, 128), 1)
    spot = lane // 32

    def pack(t, res):
        for h in range(2):
            part = [res[:, c, :, h * 128 : (h + 1) * 128].reshape(32, 128) for c in range(3)]
            one = pltpu.roll(part[1], 32, 1)
            two = pltpu.roll(part[2], 64, 1)
            for g in range(4):
                tile = jnp.where(
                    spot == (g + 1) % 4, one, jnp.where(spot == (g + 2) % 4, two, part[0])
                )
                for half in range(2):
                    rows = jnp.concatenate(
                        (tile[half * 8 : half * 8 + 8], tile[16 + half * 8 : 24 + half * 8]), axis=0
                    )
                    sb[t, h * 4 + g, half] = rows.astype(BF)

    slot = lax.rem(w // 8, 2) * 16 + (w // 16) * 8 + lax.rem(w, 8)
    half_sem = rsem1.at[lax.rem(w // 8, 2)]

    def send(t):
        for g in range(8):
            to = worker_of(t, g)

            @pl.when(w != to)
            def _():
                pltpu.make_async_remote_copy(
                    src_ref=sb.at[t, g], dst_ref=rv1.at[slot], send_sem=ssem1, recv_sem=half_sem,
                    device_id={"wheel": to}, device_id_type=MESH,
                ).start()

            @pl.when(w == to)
            def _():
                pltpu.make_async_copy(sb.at[t, g], rv1.at[slot], half_sem).start()

    pack(0, v - shift_value * u)
    send(0)

    def stencil(ke, k, picked):
        picked = picked.reshape(2, 3, 16, 256)
        for c in range(3):
            for d in range(3):
                ke[c] = ke[c] + st[c, d, k : k + 1, :] * picked[:, d]
        return ke

    for load in loads[3:7]:
        load.wait()
    own = jnp.concatenate((ehi, elo), axis=0)
    ke = [jnp.zeros((2, 16, 256), F32) for _ in range(3)]
    for k in range(8):
        both = jnp.dot(own, one_hot(256, 256, nb[k : k + 1, :]), preferred_element_type=F32)
        ke = stencil(ke, k, both[:96] + both[96:])

    @pl.when(has_up)
    def _():
        halos[0].wait_send()
        halos[1].wait_recv()

    @pl.when(jnp.logical_not(has_up))
    def _():
        hr[1] = jnp.zeros((96, 128), BF)

    @pl.when(has_down)
    def _():
        halos[1].wait_send()
        halos[0].wait_recv()

    @pl.when(jnp.logical_not(has_down))
    def _():
        hr[0] = jnp.zeros((96, 128), BF)

    halos[2].wait()
    halos[3].wait()
    iface = hr[0].astype(F32) + hr[1].astype(F32)
    face = jnp.concatenate(
        (
            hrw[0].astype(F32) + picks[48:96, 384:512],
            hrw[1].astype(F32) + picks[0:48, 256:384],
        ),
        axis=0,
    )
    halo = jnp.concatenate((iface, face), axis=1).astype(BF)
    for k in range(8):
        ke = stencil(
            ke, k, jnp.dot(halo, one_hot(256, 256, nb[k : k + 1, :] - 256), preferred_element_type=F32)
        )

    mass = [ms[c : c + 1, :] for c in range(3)]
    gyro = (-(mass[0] * v[:, 1]), mass[1] * v[:, 0], None)
    rows = []
    for c in range(3):
        scaled = jnp.stack(
            [(1.0 + class_step * bc[s].astype(F32)) * ke[c][s] for s in range(2)], axis=0
        )
        row = -scaled - shift_value * (mass[c] * v[:, c])
        if c < 2:
            row = row - gyro_rate * gyro[c]
        rows.append(row)
    pack(1, jnp.stack(rows, axis=1))
    send(1)

    def sent(count, sem):
        whole = rv1.at[pl.ds(0, count)]
        pltpu.make_async_copy(whole, whole, sem).wait()

    @pl.when(works)
    def _():
        loads[7].wait()

        def field(part):
            both = rv1[part * 16 : part * 16 + 16]
            return jnp.concatenate(
                (both[:, 0].reshape(256, 128), both[:, 1].reshape(256, 128)), axis=1
            )

        def transform(first, part, data):
            rows = slice(first * 256, first * 256 + 256)
            cols = slice(part * 256, part * 256 + 256)
            return jnp.dot(kmv[0, rows, cols], data, preferred_element_type=F32) + jnp.dot(
                kmv[1, rows, cols], data, preferred_element_type=F32
            )

        def arrived(part):
            whole = rv1.at[pl.ds(part * 16, 16)]
            pltpu.make_async_copy(whole, whole, rsem1.at[part]).wait()

        def answer(to, group):
            @pl.when(w != to)
            def _():
                pltpu.make_async_remote_copy(
                    src_ref=sb2.at[to], dst_ref=rv2.at[my_t, my_g], send_sem=ssem2.at[group],
                    recv_sem=rsem2.at[my_t], device_id={"wheel": to}, device_id_type=MESH,
                ).start()

            @pl.when(w == to)
            def _():
                pltpu.make_async_copy(sb2.at[to], rv2.at[my_t, my_g], rsem2.at[my_t]).start()

        def left(group):
            mine = lax.rem(w // 8, 2) == group

            @pl.when(mine)
            def _():
                sent(15, ssem2.at[group])

            @pl.when(jnp.logical_not(mine))
            def _():
                sent(16, ssem2.at[group])

        arrived(0)
        near = field(0)
        for first in range(2):
            acc[first] = transform(first, 0, near)
        arrived(1)
        far = field(1)
        for first in range(2):
            har = (acc[first] + transform(first, 1, far)).reshape(16, 2, 8, 256)
            sb2[first * 16 : first * 16 + 16] = jnp.concatenate(
                (har[..., :128], har[..., 128:]), axis=2
            ).astype(BF)
            for z in range(4):
                for core in range(2):
                    answer(first * 16 + z * 2 + core, 0)

        left(0)
        for first in range(2):
            for z in (7, 4, 5, 6):
                for core in range(2):
                    answer(first * 16 + z * 2 + core, 1)

    for t in range(2):
        pltpu.make_async_copy(rv2.at[t], rv2.at[t], rsem2.at[t]).wait()
    loads[8].wait()
    lane16 = lax.broadcasted_iota(jnp.int32, (16, 128), 1)
    for g in range(8):
        turned = []
        for q in range(2):
            for t in range(2):
                x = rv2[t, g, q].astype(F32)
                shift = (96 * (2 * q + t) - 32 * (g % 4)) % 128
                turned.append(pltpu.roll(x, shift, 1) if shift else x)
        lhs = jnp.concatenate(
            (
                jnp.where(lane16 < 96, turned[0], turned[1]),
                jnp.where(lane16 < 64, turned[1], turned[2]),
                jnp.where(lane16 < 32, turned[2], turned[3]),
            ),
            axis=1,
        ).astype(BF)
        out[0, g] = lax.dot_general(
            lhs, pcv[0, g], (((1,), (1,)), ((), ())), preferred_element_type=F32
        )

    @pl.when(works)
    def _():
        sent(15, ssem1)
        mine = lax.rem(w // 8, 2) == 1

        @pl.when(mine)
        def _():
            sent(15, ssem2.at[1])

        @pl.when(jnp.logical_not(mine))
        def _():
            sent(16, ssem2.at[1])

    @pl.when(jnp.logical_not(works))
    def _():
        loads[7].wait()
        sent(16, ssem1)


def on_device(
    krylov_block, blade_class, neighbors, iface_rows, face_rows, stiffness, lumped_mass, precond
):
    vmem = pl.BlockSpec(memory_space=pltpu.VMEM)
    hbm = pl.BlockSpec(memory_space=pltpu.HBM)
    return pl.pallas_call(
        kernel,
        out_shape=jax.ShapeDtypeStruct((1, 8, 16, 384), F32),
        in_specs=[hbm] * 9,
        out_specs=vmem,
        scratch_shapes=[
            pltpu.VMEM((2, 2, 3, 16, 256), F32),
            pltpu.SMEM((2,), jnp.int32),
            pltpu.VMEM((8, 256), jnp.int32),
            pltpu.VMEM((2, 64), jnp.int32),
            pltpu.VMEM((2, 64), jnp.int32),
            pltpu.VMEM((3, 3, 8, 256), F32),
            pltpu.VMEM((3, 256), F32),
            pltpu.VMEM((1, 8, 384, 384), BF),
            pltpu.VMEM((2, 512, 512), BF),
            pltpu.VMEM((2, 96, 128), BF),
            pltpu.VMEM((2, 48, 128), BF),
            pltpu.VMEM((2, 96, 128), BF),
            pltpu.VMEM((2, 48, 128), BF),
            pltpu.VMEM((2, 8, 2, 16, 128), BF),
            pltpu.VMEM((32, 2, 16, 128), BF),
            pltpu.VMEM((2, 256, 256), F32),
            pltpu.VMEM((32, 2, 16, 128), BF),
            pltpu.VMEM((2, 8, 2, 16, 128), BF),
            pltpu.SemaphoreType.DMA((9,)),
            pltpu.SemaphoreType.DMA((4,)),
            pltpu.SemaphoreType.DMA((4,)),
            pltpu.SemaphoreType.DMA,
            pltpu.SemaphoreType.DMA((2,)),
            pltpu.SemaphoreType.DMA((2,)),
            pltpu.SemaphoreType.DMA((2,)),
        ],
        compiler_params=pltpu.CompilerParams(
            collective_id=0, has_side_effects=True, vmem_limit_bytes=40 * 1024 * 1024
        ),
    )(
        *(
            pltpu.with_memory_space_constraint(operand, pltpu.HBM)
            for operand in (
                krylov_block, blade_class, neighbors, iface_rows, face_rows, stiffness, lumped_mass,
                precond, jnp.asarray(kron_table()),
            )
        )
    )


def solution(mesh):
    return jax.shard_map(
        on_device,
        mesh=mesh,
        in_specs=(
            P(None, "wheel", None, None, "slab"),
            P("wheel"),
            P(None, "slab"),
            P(None, "slab"),
            P(None, "slab"),
            P(None, None, None, "slab"),
            P(None, "slab"),
            P("wheel", "slab", None, None),
        ),
        out_specs=P("wheel", "slab", None, None),
        check_vma=False,
    )
```

```python
import math

import jax
import jax.numpy as jnp
import numpy as np
from jax import lax
from jax.experimental import pallas as pl
from jax.experimental.pallas import tpu as pltpu
from jax.sharding import PartitionSpec as P

import ml_dtypes

damping_ratio = 0.5
gyro_rate = 0.8
shift_value = 0.3
class_step = 0.125

SECT = 64
WHEEL = 32
SLAB = 8
MESH = pl.DeviceIdType.MESH
BF = jnp.bfloat16
F32 = jnp.float32


def slot_of(w):
    return (w // 8 % 2) * 16 + (w // 16) * 8 + w % 8


def worker_of(t, g):
    return (g // 4) * 16 + (g % 4) * 2 + t


def basis_table():
    b = np.arange(SECT)[:, None]
    s = np.arange(SECT)[None, :]
    p, q = b // 2, b % 2
    angle = 2.0 * math.pi / SECT * ((p * s) % SECT)
    inner = np.where(q == 0, np.cos(angle), np.sin(angle)) * math.sqrt(2.0 / SECT)
    edge = np.where(q == 0, 1.0, 1.0 - 2.0 * (s % 2)) * math.sqrt(1.0 / SECT)
    return np.where(p == 0, edge, inner).astype(np.float32)


def kron_table():
    sectors = [2 * w + part for w in sorted(range(WHEEL), key=slot_of) for part in range(2)]
    full = np.kron(basis_table()[:, sectors], np.eye(8, dtype=np.float32))
    high = full.astype(ml_dtypes.bfloat16)
    low = (full - high.astype(np.float32)).astype(ml_dtypes.bfloat16)
    return np.stack((high, low))


def one_hot(rows, cols, index_row):
    at = lax.broadcasted_iota(jnp.int32, (rows, cols), 0)
    return jnp.where(at == index_row, 1.0, 0.0).astype(BF)


def kernel(
    kb_hbm, bc_hbm, nb_hbm, ifr_hbm, fcr_hbm, st_hbm, ms_hbm, pc_hbm, km_hbm, out,
    kb, bc, nb, ifr, fcr, st, ms, pcv, kmv, hs, hsw, hr, hrw, sb, rv1, acc, sb2, rv2, hot, base, flip,
    lsem, hsend, hrecv, ssem1, rsem1, ssem2, rsem2,
):
    w = lax.axis_index("wheel")
    j = lax.axis_index("slab")

    up = lax.rem(j + 1, SLAB)
    down = lax.rem(j + SLAB - 1, SLAB)
    nxt = lax.rem(w + 1, WHEEL)
    prv = lax.rem(w + WHEEL - 1, WHEEL)
    loads = [
        pltpu.make_async_copy(src, dst, lsem.at[n])
        for n, (src, dst) in enumerate(
            (
                (kb_hbm, kb), (ifr_hbm, ifr), (fcr_hbm, fcr), (nb_hbm, nb), (st_hbm, st),
                (ms_hbm, ms), (bc_hbm, bc), (km_hbm, kmv), (pc_hbm, pcv),
            )
        )
    ]
    for load in loads:
        load.start()

    barrier = pltpu.get_barrier_semaphore()
    has_up = j < SLAB - 1
    has_down = j > 0

    def greet(to):
        pl.semaphore_signal(barrier, inc=1, device_id=to, device_id_type=MESH)

    @pl.when(has_up)
    def _():
        greet({"slab": up})

    @pl.when(has_down)
    def _():
        greet({"slab": down})

    greet({"wheel": nxt})
    greet({"wheel": prv})

    my_t = lax.rem(w, 2)
    along = lax.rem(w // 2, 8)
    my_g = (w // 16) * 4 + along
    works = along < 4

    @pl.when(works)
    def _():
        @pl.loop(1, WHEEL)
        def _(i):
            greet({"wheel": lax.rem(w + i, WHEEL)})

    for load in loads[:3]:
        load.wait()
    u = kb[0]
    v = kb[1]
    e = (u + damping_ratio * v).reshape(96, 256)
    ehi = e.astype(BF)
    elo = (e - ehi.astype(F32)).astype(BF)

    none = jnp.full((1, 64), -1, jnp.int32)
    index = jnp.concatenate(
        (ifr[1:2, :], none, none, ifr[0:1, :], fcr[1:2, :], none, none, fcr[0:1, :]), axis=1
    )
    picks = jnp.dot(ehi, one_hot(256, 512, index), preferred_element_type=F32)
    hs[0] = picks[:, 0:128].astype(BF)
    hs[1] = picks[:, 128:256].astype(BF)
    hsw[0] = picks[48:96, 256:384].astype(BF)
    hsw[1] = picks[0:48, 384:512].astype(BF)

    pl.semaphore_wait(
        barrier,
        18 + jnp.where(has_up, 1, 0) + jnp.where(has_down, 1, 0) - jnp.where(works, 1, 0),
    )

    halos = [
        pltpu.make_async_remote_copy(
            src_ref=src, dst_ref=dst, send_sem=hsend.at[n], recv_sem=hrecv.at[n],
            device_id=to, device_id_type=MESH,
        )
        for n, (src, dst, to) in enumerate(
            (
                (hs.at[0], hr.at[0], {"slab": up}),
                (hs.at[1], hr.at[1], {"slab": down}),
                (hsw.at[0], hrw.at[0], {"wheel": nxt}),
                (hsw.at[1], hrw.at[1], {"wheel": prv}),
            )
        )
    ]

    @pl.when(has_up)
    def _():
        halos[0].start()

    @pl.when(has_down)
    def _():
        halos[1].start()

    halos[2].start()
    halos[3].start()

    lane = lax.broadcasted_iota(jnp.int32, (32, 128), 1)
    spot = lane // 32

    def pack(t, res):
        for h in range(2):
            part = [res[:, c, :, h * 128 : (h + 1) * 128].reshape(32, 128) for c in range(3)]
            one = pltpu.roll(part[1], 32, 1)
            two = pltpu.roll(part[2], 64, 1)
            for g in range(4):
                tile = jnp.where(
                    spot == (g + 1) % 4, one, jnp.where(spot == (g + 2) % 4, two, part[0])
                )
                for half in range(2):
                    rows = jnp.concatenate(
                        (tile[half * 8 : half * 8 + 8], tile[16 + half * 8 : 24 + half * 8]), axis=0
                    )
                    sb[t, h * 4 + g, half] = rows.astype(BF)

    slot = lax.rem(w // 8, 2) * 16 + (w // 16) * 8 + lax.rem(w, 8)
    half_sem = rsem1.at[lax.rem(w // 8, 2)]

    def send(t):
        for g in range(8):
            to = worker_of(t, g)

            @pl.when(w != to)
            def _():
                pltpu.make_async_remote_copy(
                    src_ref=sb.at[t, g], dst_ref=rv1.at[slot], send_sem=ssem1, recv_sem=half_sem,
                    device_id={"wheel": to}, device_id_type=MESH,
                ).start()

            @pl.when(w == to)
            def _():
                pltpu.make_async_copy(sb.at[t, g], rv1.at[slot], half_sem).start()

    pack(0, v - shift_value * u)
    send(0)

    def stencil(ke, k, picked):
        picked = picked.reshape(2, 3, 16, 256)
        for c in range(3):
            for d in range(3):
                ke[c] = ke[c] + st[c, d, k : k + 1, :] * picked[:, d]
        return ke

    for load in loads[3:7]:
        load.wait()
    own = jnp.concatenate((ehi, elo), axis=0)
    ke = [jnp.zeros((2, 16, 256), F32) for _ in range(3)]
    for k in range(8):
        both = jnp.dot(own, one_hot(256, 256, nb[k : k + 1, :]), preferred_element_type=F32)
        ke = stencil(ke, k, both[:96] + both[96:])

    for k in range(8):
        hot[k] = one_hot(256, 256, nb[k : k + 1, :] - 256)
    mass = [ms[c : c + 1, :] for c in range(3)]
    gyro = (-(mass[0] * v[:, 1]), mass[1] * v[:, 0], None)
    scale = [1.0 + class_step * bc[s].astype(F32) for s in range(2)]

    def scaled(part):
        return jnp.stack([scale[s] * part[s] for s in range(2)], axis=0)

    for c in range(3):
        row = -scaled(ke[c]) - shift_value * (mass[c] * v[:, c])
        if c < 2:
            row = row - gyro_rate * gyro[c]
        base[c] = row

    @pl.when(has_up)
    def _():
        halos[0].wait_send()
        halos[1].wait_recv()

    @pl.when(jnp.logical_not(has_up))
    def _():
        hr[1] = jnp.zeros((96, 128), BF)

    @pl.when(has_down)
    def _():
        halos[1].wait_send()
        halos[0].wait_recv()

    @pl.when(jnp.logical_not(has_down))
    def _():
        hr[0] = jnp.zeros((96, 128), BF)

    halos[2].wait()
    halos[3].wait()
    iface = hr[0].astype(F32) + hr[1].astype(F32)
    face = jnp.concatenate(
        (
            hrw[0].astype(F32) + picks[48:96, 384:512],
            hrw[1].astype(F32) + picks[0:48, 256:384],
        ),
        axis=0,
    )
    halo = jnp.concatenate((iface, face), axis=1).astype(BF)
    ke = [jnp.zeros((2, 16, 256), F32) for _ in range(3)]
    for k in range(8):
        ke = stencil(ke, k, jnp.dot(halo, hot[k], preferred_element_type=F32))
    rows = [base[c] - scaled(ke[c]) for c in range(3)]
    pack(1, jnp.stack(rows, axis=1))
    send(1)

    def sent(count, sem):
        whole = rv1.at[pl.ds(0, count)]
        pltpu.make_async_copy(whole, whole, sem).wait()

    @pl.when(works)
    def _():
        loads[7].wait()

        def field(part):
            both = rv1[part * 16 : part * 16 + 16]
            return jnp.concatenate(
                (both[:, 0].reshape(256, 128), both[:, 1].reshape(256, 128)), axis=1
            )

        def transform(first, part, data):
            rows = slice(first * 256, first * 256 + 256)
            cols = slice(part * 256, part * 256 + 256)
            return jnp.dot(kmv[0, rows, cols], data, preferred_element_type=F32) + jnp.dot(
                kmv[1, rows, cols], data, preferred_element_type=F32
            )

        def arrived(part):
            whole = rv1.at[pl.ds(part * 16, 16)]
            pltpu.make_async_copy(whole, whole, rsem1.at[part]).wait()

        def answer(to, group):
            @pl.when(w != to)
            def _():
                pltpu.make_async_remote_copy(
                    src_ref=sb2.at[to], dst_ref=rv2.at[my_t, my_g], send_sem=ssem2.at[group],
                    recv_sem=rsem2.at[my_t], device_id={"wheel": to}, device_id_type=MESH,
                ).start()

            @pl.when(w == to)
            def _():
                pltpu.make_async_copy(sb2.at[to], rv2.at[my_t, my_g], rsem2.at[my_t]).start()

        arrived(0)
        near = field(0)
        for first in range(2):
            acc[first] = transform(first, 0, near)
        arrived(1)
        far = field(1)
        for first in range(2):
            har = (acc[first] + transform(first, 1, far)).reshape(16, 2, 8, 256)
            sb2[first * 16 : first * 16 + 16] = jnp.concatenate(
                (har[..., :128], har[..., 128:]), axis=2
            ).astype(BF)
            for z in range(4):
                for core in range(2):
                    answer(first * 16 + z * 2 + core, 0)

        sent(15, ssem2.at[0])
        for first in range(2):
            for z in (7, 4, 5, 6):
                for core in range(2):
                    answer(first * 16 + z * 2 + core, 1)

    loads[8].wait()
    for g in range(8):
        turned = pcv[0, g].T
        flip[g, 0:96] = turned[96:192]
        flip[g, 96:192] = turned[288:384]

    lane16 = lax.broadcasted_iota(jnp.int32, (16, 128), 1)
    zero = jnp.zeros((16, 128), F32)

    def placed(t, g, q, at):
        shift = (at - 32 * (g % 4)) % 128
        x = rv2[t, g, q].astype(F32)
        return pltpu.roll(x, shift, 1) if shift else x

    pltpu.make_async_copy(rv2.at[0], rv2.at[0], rsem2.at[0]).wait()
    for g in range(8):
        low = jnp.where(lane16 < 96, placed(0, g, 0, 0), zero)
        top = placed(0, g, 1, 64)
        lhs = jnp.concatenate(
            (low, jnp.where(lane16 >= 64, top, zero), jnp.where(lane16 < 32, top, zero)), axis=1
        ).astype(BF)
        out[0, g] = lax.dot_general(
            lhs, pcv[0, g], (((1,), (1,)), ((), ())), preferred_element_type=F32
        )

    pltpu.make_async_copy(rv2.at[1], rv2.at[1], rsem2.at[1]).wait()
    for g in range(8):
        top = placed(1, g, 1, 96)
        lhs = jnp.concatenate(
            (jnp.where(lane16 < 96, placed(1, g, 0, 0), top), top), axis=1
        ).astype(BF)
        out[0, g] += jnp.dot(lhs[:, :192], flip[g], preferred_element_type=F32)

    @pl.when(works)
    def _():
        sent(15, ssem1)
        sent(16, ssem2.at[1])

    @pl.when(jnp.logical_not(works))
    def _():
        loads[7].wait()
        sent(16, ssem1)


def on_device(
    krylov_block, blade_class, neighbors, iface_rows, face_rows, stiffness, lumped_mass, precond
):
    vmem = pl.BlockSpec(memory_space=pltpu.VMEM)
    hbm = pl.BlockSpec(memory_space=pltpu.HBM)
    return pl.pallas_call(
        kernel,
        out_shape=jax.ShapeDtypeStruct((1, 8, 16, 384), F32),
        in_specs=[hbm] * 9,
        out_specs=vmem,
        scratch_shapes=[
            pltpu.VMEM((2, 2, 3, 16, 256), F32),
            pltpu.SMEM((2,), jnp.int32),
            pltpu.VMEM((8, 256), jnp.int32),
            pltpu.VMEM((2, 64), jnp.int32),
            pltpu.VMEM((2, 64), jnp.int32),
            pltpu.VMEM((3, 3, 8, 256), F32),
            pltpu.VMEM((3, 256), F32),
            pltpu.VMEM((1, 8, 384, 384), BF),
            pltpu.VMEM((2, 512, 512), BF),
            pltpu.VMEM((2, 96, 128), BF),
            pltpu.VMEM((2, 48, 128), BF),
            pltpu.VMEM((2, 96, 128), BF),
            pltpu.VMEM((2, 48, 128), BF),
            pltpu.VMEM((2, 8, 2, 16, 128), BF),
            pltpu.VMEM((32, 2, 16, 128), BF),
            pltpu.VMEM((2, 256, 256), F32),
            pltpu.VMEM((32, 2, 16, 128), BF),
            pltpu.VMEM((2, 8, 2, 16, 128), BF),
            pltpu.VMEM((8, 256, 256), BF),
            pltpu.VMEM((3, 2, 16, 256), F32),
            pltpu.VMEM((8, 192, 384), BF),
            pltpu.SemaphoreType.DMA((9,)),
            pltpu.SemaphoreType.DMA((4,)),
            pltpu.SemaphoreType.DMA((4,)),
            pltpu.SemaphoreType.DMA,
            pltpu.SemaphoreType.DMA((2,)),
            pltpu.SemaphoreType.DMA((2,)),
            pltpu.SemaphoreType.DMA((2,)),
        ],
        compiler_params=pltpu.CompilerParams(
            collective_id=0, has_side_effects=True, vmem_limit_bytes=40 * 1024 * 1024
        ),
    )(
        *(
            pltpu.with_memory_space_constraint(operand, pltpu.HBM)
            for operand in (
                krylov_block, blade_class, neighbors, iface_rows, face_rows, stiffness, lumped_mass,
                precond, jnp.asarray(kron_table()),
            )
        )
    )


def solution(mesh):
    return jax.shard_map(
        on_device,
        mesh=mesh,
        in_specs=(
            P(None, "wheel", None, None, "slab"),
            P("wheel"),
            P(None, "slab"),
            P(None, "slab"),
            P(None, "slab"),
            P(None, None, None, "slab"),
            P(None, "slab"),
            P("wheel", "slab", None, None),
        ),
        out_specs=P("wheel", "slab", None, None),
        check_vma=False,
    )
```

```python
import math

import jax
import jax.numpy as jnp
import numpy as np
from jax import lax
from jax.experimental import pallas as pl
from jax.experimental.pallas import tpu as pltpu
from jax.sharding import PartitionSpec as P

import ml_dtypes

damping_ratio = 0.5
gyro_rate = 0.8
shift_value = 0.3
class_step = 0.125

SECT = 64
WHEEL = 32
SLAB = 8
MESH = pl.DeviceIdType.MESH
BF = jnp.bfloat16
F32 = jnp.float32


def slot_of(w):
    return (w // 8 % 2) * 16 + (w // 16) * 8 + w % 8


def worker_of(t, g):
    return (g // 4) * 16 + (g % 4) * 2 + t


def basis_table():
    b = np.arange(SECT)[:, None]
    s = np.arange(SECT)[None, :]
    p, q = b // 2, b % 2
    angle = 2.0 * math.pi / SECT * ((p * s) % SECT)
    inner = np.where(q == 0, np.cos(angle), np.sin(angle)) * math.sqrt(2.0 / SECT)
    edge = np.where(q == 0, 1.0, 1.0 - 2.0 * (s % 2)) * math.sqrt(1.0 / SECT)
    return np.where(p == 0, edge, inner).astype(np.float32)


def kron_table():
    sectors = [2 * w + part for w in sorted(range(WHEEL), key=slot_of) for part in range(2)]
    full = np.kron(basis_table()[:, sectors], np.eye(8, dtype=np.float32))
    high = full.astype(ml_dtypes.bfloat16)
    low = (full - high.astype(np.float32)).astype(ml_dtypes.bfloat16)
    return np.stack((high, low))


def one_hot(rows, cols, index_row):
    at = lax.broadcasted_iota(jnp.int32, (rows, cols), 0)
    return jnp.where(at == index_row, 1.0, 0.0).astype(BF)


def kernel(
    kb_hbm, bc_hbm, nb_hbm, ifr_hbm, fcr_hbm, st_hbm, ms_hbm, pc_hbm, km_hbm, out,
    kb, bc, nb, ifr, fcr, st, ms, pcv, kmv, hs, hsw, hr, hrw, sb, rv1, acc, sb2, rv2, hot, base, flip, pick_hot,
    ready, lsem, hsend, hrecv, ssem1, rsem1, ssem2, rsem2,
):
    w = lax.axis_index("wheel")
    j = lax.axis_index("slab")

    up = lax.rem(j + 1, SLAB)
    down = lax.rem(j + SLAB - 1, SLAB)
    nxt = lax.rem(w + 1, WHEEL)
    prv = lax.rem(w + WHEEL - 1, WHEEL)
    loads = [
        pltpu.make_async_copy(src, dst, lsem.at[n])
        for n, (src, dst) in enumerate(
            (
                (ifr_hbm, ifr), (fcr_hbm, fcr),
                *((kb_hbm.at[t, p], kb.at[t, p]) for p in range(2) for t in range(2)),
                (nb_hbm, nb), (st_hbm, st), (ms_hbm, ms), (bc_hbm, bc), (km_hbm, kmv), (pc_hbm, pcv),
            )
        )
    ]
    for load in loads:
        load.start()

    barrier = pltpu.get_barrier_semaphore()
    has_up = j < SLAB - 1
    has_down = j > 0

    def greet(to):
        pl.semaphore_signal(barrier, inc=1, device_id=to, device_id_type=MESH)

    @pl.when(has_up)
    def _():
        greet({"slab": up})

    @pl.when(has_down)
    def _():
        greet({"slab": down})

    greet({"wheel": nxt})
    greet({"wheel": prv})

    my_t = lax.rem(w, 2)
    along = lax.rem(w // 2, 8)
    my_g = (w // 16) * 4 + along
    works = along < 4

    late = jnp.logical_not(works)

    @pl.when(works)
    def _():
        mine = (w // 16) * 8 + lax.rem(w, 8)

        @pl.loop(1, 16)
        def _(i):
            other = lax.rem(mine + i, 16)
            greet({"wheel": (other // 8) * 16 + lax.rem(other, 8)})

    @pl.when(late)
    def _():
        greet({"wheel": w - 2 * jnp.where(along == 7, 7, along - 3)})

    for load in loads[:2]:
        load.wait()
    none = jnp.full((1, 64), -1, jnp.int32)
    index = jnp.concatenate(
        (ifr[1:2, :], none, none, ifr[0:1, :], fcr[1:2, :], none, none, fcr[0:1, :]), axis=1
    )
    pick_hot[...] = one_hot(256, 512, index)
    for load in loads[2:6]:
        load.wait()
    u = kb[0]
    v = kb[1]
    e = (u + damping_ratio * v).reshape(96, 256)
    ehi = e.astype(BF)
    elo = (e - ehi.astype(F32)).astype(BF)

    picks = jnp.dot(ehi, pick_hot[...], preferred_element_type=F32)
    hs[0] = (picks[0:48, 0:128] + pltpu.roll(picks[48:96, 0:128], 64, 1)).astype(BF)
    hs[1] = (pltpu.roll(picks[0:48, 128:256], 64, 1) + picks[48:96, 128:256]).astype(BF)
    hsw[0] = picks[48:96, 256:384].astype(BF)
    hsw[1] = picks[0:48, 384:512].astype(BF)

    greeted = 15 + jnp.where(along == 3, 3, 0) + jnp.where(along == 0, 1, 0)
    pl.semaphore_wait(
        barrier,
        2 + jnp.where(has_up, 1, 0) + jnp.where(has_down, 1, 0) + jnp.where(works, greeted, 0),
    )

    def tell(to):
        pl.semaphore_signal(ready, inc=1, device_id={"wheel": to}, device_id_type=MESH)

    @pl.when(along == 3)
    def _():
        for step in (2, 4, 6):
            tell(w + step)

    @pl.when(along == 0)
    def _():
        tell(w + 14)

    halos = [
        pltpu.make_async_remote_copy(
            src_ref=src, dst_ref=dst, send_sem=hsend.at[n], recv_sem=hrecv.at[n],
            device_id=to, device_id_type=MESH,
        )
        for n, (src, dst, to) in enumerate(
            (
                (hs.at[0], hr.at[0], {"slab": up}),
                (hs.at[1], hr.at[1], {"slab": down}),
                (hsw.at[0], hrw.at[0], {"wheel": nxt}),
                (hsw.at[1], hrw.at[1], {"wheel": prv}),
            )
        )
    ]

    @pl.when(has_up)
    def _():
        halos[0].start()

    @pl.when(has_down)
    def _():
        halos[1].start()

    halos[2].start()
    halos[3].start()

    lane = lax.broadcasted_iota(jnp.int32, (32, 128), 1)
    spot = lane // 32

    def squeeze(a, b, c, d, spare):
        turned = [pltpu.roll(d, shift, d.ndim - 1) for shift in (96, 64, 32)]
        return jnp.concatenate(
            [jnp.where(spare, x, y) for x, y in zip(turned, (a, b, c))], axis=-2
        )

    def fourth(a, b, c, place, first):
        axis = a.ndim - 1
        return jnp.where(
            place == first,
            pltpu.roll(a, 32, axis),
            jnp.where(place == lax.rem(first + 1, 4), pltpu.roll(b, 64, axis), pltpu.roll(c, 96, axis)),
        )

    def pack(t, res):
        for h in range(2):
            part = [res[:, c, :, h * 128 : (h + 1) * 128].reshape(32, 128) for c in range(3)]
            one = pltpu.roll(part[1], 32, 1)
            two = pltpu.roll(part[2], 64, 1)
            for g in range(4):
                tile = jnp.where(
                    spot == (g + 1) % 4, one, jnp.where(spot == (g + 2) % 4, two, part[0])
                )
                sb[t, h * 4 + g] = squeeze(
                    tile[0:8], tile[16:24], tile[8:16], tile[24:32], spot[:8] == (g + 3) % 4
                ).astype(BF)

    slot = lax.rem(w // 8, 2) * 16 + (w // 16) * 8 + lax.rem(w, 8)
    half_sem = rsem1.at[lax.rem(w // 8, 2)]

    def send(t):
        for g in range(8):
            to = worker_of(t, g)

            @pl.when(w != to)
            def _():
                pltpu.make_async_remote_copy(
                    src_ref=sb.at[t, g], dst_ref=rv1.at[slot], send_sem=ssem1, recv_sem=half_sem,
                    device_id={"wheel": to}, device_id_type=MESH,
                ).start()

            @pl.when(w == to)
            def _():
                pltpu.make_async_copy(sb.at[t, g], rv1.at[slot], half_sem).start()

    pack(0, v - shift_value * u)

    @pl.when(works)
    def _():
        send(0)

    def stencil(ke, k, picked):
        picked = picked.reshape(2, 3, 16, 256)
        for c in range(3):
            for d in range(3):
                ke[c] = ke[c] + st[c, d, k : k + 1, :] * picked[:, d]
        return ke

    for load in loads[6:10]:
        load.wait()
    own = jnp.concatenate((ehi, elo), axis=0)
    ke = [jnp.zeros((2, 16, 256), F32) for _ in range(3)]
    for k in range(8):
        both = jnp.dot(own, one_hot(256, 256, nb[k : k + 1, :]), preferred_element_type=F32)
        ke = stencil(ke, k, both[:96] + both[96:])

    for k in range(8):
        hot[k] = one_hot(256, 256, nb[k : k + 1, :] - 256)
    mass = [ms[c : c + 1, :] for c in range(3)]
    gyro = (-(mass[0] * v[:, 1]), mass[1] * v[:, 0], None)
    scale = [1.0 + class_step * bc[s].astype(F32) for s in range(2)]

    def scaled(part):
        return jnp.stack([scale[s] * part[s] for s in range(2)], axis=0)

    for c in range(3):
        row = -scaled(ke[c]) - shift_value * (mass[c] * v[:, c])
        if c < 2:
            row = row - gyro_rate * gyro[c]
        base[c] = row

    @pl.when(late)
    def _():
        pl.semaphore_wait(ready, 1)
        send(0)

    @pl.when(has_up)
    def _():
        halos[0].wait_send()
        halos[1].wait_recv()

    @pl.when(jnp.logical_not(has_up))
    def _():
        hr[1] = jnp.zeros((48, 128), BF)

    @pl.when(has_down)
    def _():
        halos[1].wait_send()
        halos[0].wait_recv()

    @pl.when(jnp.logical_not(has_down))
    def _():
        hr[0] = jnp.zeros((48, 128), BF)

    halos[2].wait()
    halos[3].wait()
    lower, upper = hr[0].astype(F32), hr[1].astype(F32)
    left_half = lax.broadcasted_iota(jnp.int32, (48, 128), 1) < 64
    iface = jnp.concatenate(
        (
            jnp.where(left_half, lower, pltpu.roll(upper, 64, 1)),
            jnp.where(left_half, pltpu.roll(lower, 64, 1), upper),
        ),
        axis=0,
    )
    face = jnp.concatenate(
        (
            hrw[0].astype(F32) + picks[48:96, 384:512],
            hrw[1].astype(F32) + picks[0:48, 256:384],
        ),
        axis=0,
    )
    halo = jnp.concatenate((iface, face), axis=1).astype(BF)
    ke = [jnp.zeros((2, 16, 256), F32) for _ in range(3)]
    for k in range(8):
        ke = stencil(ke, k, jnp.dot(halo, hot[k], preferred_element_type=F32))
    rows = [base[c] - scaled(ke[c]) for c in range(3)]
    pack(1, jnp.stack(rows, axis=1))
    send(1)

    def sent(count, sem):
        whole = rv1.at[pl.ds(0, count)]
        pltpu.make_async_copy(whole, whole, sem).wait()

    @pl.when(works)
    def _():
        loads[10].wait()

        corner = lax.rem(my_g, 4)
        place = lax.broadcasted_iota(jnp.int32, (16, 8, 128), 2) // 32

        def field(part):
            got = rv1[part * 16 : part * 16 + 16].astype(F32)
            a, b, c = (got[:, n * 8 : n * 8 + 8] for n in range(3))
            d = fourth(a, b, c, place, corner)
            return jnp.concatenate(
                [
                    jnp.concatenate(pair, axis=1).astype(BF).reshape(256, 128)
                    for pair in ((a, b), (c, d))
                ],
                axis=1,
            )

        def transform(first, part, data):
            rows = slice(first * 256, first * 256 + 256)
            cols = slice(part * 256, part * 256 + 256)
            return jnp.dot(kmv[0, rows, cols], data, preferred_element_type=F32) + jnp.dot(
                kmv[1, rows, cols], data, preferred_element_type=F32
            )

        def arrived(part):
            whole = rv1.at[pl.ds(part * 16, 16)]
            pltpu.make_async_copy(whole, whole, rsem1.at[part]).wait()

        def answer(to, group):
            @pl.when(w != to)
            def _():
                pltpu.make_async_remote_copy(
                    src_ref=sb2.at[to], dst_ref=rv2.at[my_t, my_g], send_sem=ssem2.at[group],
                    recv_sem=rsem2.at[my_t], device_id={"wheel": to}, device_id_type=MESH,
                ).start()

            @pl.when(w == to)
            def _():
                pltpu.make_async_copy(sb2.at[to], rv2.at[my_t, my_g], rsem2.at[my_t]).start()

        arrived(0)
        near = field(0)
        for first in range(2):
            acc[first] = transform(first, 0, near)
        arrived(1)
        far = field(1)
        for first in range(2):
            har = (acc[first] + transform(first, 1, far)).reshape(16, 2, 8, 256)
            sb2[first * 16 : first * 16 + 16] = squeeze(
                har[:, 0, :, :128], har[:, 0, :, 128:], har[:, 1, :, :128], har[:, 1, :, 128:],
                place == lax.rem(corner + 3, 4),
            ).astype(BF)
            for z in (0, 1, 2, 3):
                for core in range(2):
                    answer(first * 16 + z * 2 + core, 0)

        sent(15, ssem2.at[0])
        for first in range(2):
            for z in (7, 4, 5, 6):
                for core in range(2):
                    answer(first * 16 + z * 2 + core, 1)

    loads[11].wait()
    for g in range(8):
        turned = pcv[0, g].T
        flip[g, 0:96] = turned[96:192]
        flip[g, 96:192] = turned[288:384]

    lane16 = lax.broadcasted_iota(jnp.int32, (16, 128), 1)
    zero = jnp.zeros((16, 128), F32)

    def placed(t, g, q, at):
        shift = (at - 32 * (g % 4)) % 128
        got = rv2[t, g].astype(F32)
        if q == 0:
            x = got[:16]
        else:
            last = fourth(got[:8], got[8:16], got[16:], lane16[:8] // 32, g % 4)
            x = jnp.concatenate((got[16:], last), axis=0)
        return pltpu.roll(x, shift, 1) if shift else x

    pltpu.make_async_copy(rv2.at[0], rv2.at[0], rsem2.at[0]).wait()
    for g in range(8):
        low = jnp.where(lane16 < 96, placed(0, g, 0, 0), zero)
        top = placed(0, g, 1, 64)
        lhs = jnp.concatenate(
            (low, jnp.where(lane16 >= 64, top, zero), jnp.where(lane16 < 32, top, zero)), axis=1
        ).astype(BF)
        out[0, g] = lax.dot_general(
            lhs, pcv[0, g], (((1,), (1,)), ((), ())), preferred_element_type=F32
        )

    pltpu.make_async_copy(rv2.at[1], rv2.at[1], rsem2.at[1]).wait()
    for g in range(8):
        top = placed(1, g, 1, 96)
        lhs = jnp.concatenate(
            (jnp.where(lane16 < 96, placed(1, g, 0, 0), top), top), axis=1
        ).astype(BF)
        out[0, g] += jnp.dot(lhs[:, :192], flip[g], preferred_element_type=F32)

    @pl.when(works)
    def _():
        sent(15, ssem1)
        sent(16, ssem2.at[1])

    @pl.when(late)
    def _():
        loads[10].wait()
        sent(16, ssem1)


def on_device(
    krylov_block, blade_class, neighbors, iface_rows, face_rows, stiffness, lumped_mass, precond
):
    vmem = pl.BlockSpec(memory_space=pltpu.VMEM)
    hbm = pl.BlockSpec(memory_space=pltpu.HBM)
    return pl.pallas_call(
        kernel,
        out_shape=jax.ShapeDtypeStruct((1, 8, 16, 384), F32),
        in_specs=[hbm] * 9,
        out_specs=vmem,
        scratch_shapes=[
            pltpu.VMEM((2, 2, 3, 16, 256), F32),
            pltpu.SMEM((2,), jnp.int32),
            pltpu.VMEM((8, 256), jnp.int32),
            pltpu.VMEM((2, 64), jnp.int32),
            pltpu.VMEM((2, 64), jnp.int32),
            pltpu.VMEM((3, 3, 8, 256), F32),
            pltpu.VMEM((3, 256), F32),
            pltpu.VMEM((1, 8, 384, 384), BF),
            pltpu.VMEM((2, 512, 512), BF),
            pltpu.VMEM((2, 48, 128), BF),
            pltpu.VMEM((2, 48, 128), BF),
            pltpu.VMEM((2, 48, 128), BF),
            pltpu.VMEM((2, 48, 128), BF),
            pltpu.VMEM((2, 8, 24, 128), BF),
            pltpu.VMEM((32, 24, 128), BF),
            pltpu.VMEM((2, 256, 256), F32),
            pltpu.VMEM((32, 24, 128), BF),
            pltpu.VMEM((2, 8, 24, 128), BF),
            pltpu.VMEM((8, 256, 256), BF),
            pltpu.VMEM((3, 2, 16, 256), F32),
            pltpu.VMEM((8, 192, 384), BF),
            pltpu.VMEM((256, 512), BF),
            pltpu.SemaphoreType.REGULAR,
            pltpu.SemaphoreType.DMA((12,)),
            pltpu.SemaphoreType.DMA((4,)),
            pltpu.SemaphoreType.DMA((4,)),
            pltpu.SemaphoreType.DMA,
            pltpu.SemaphoreType.DMA((2,)),
            pltpu.SemaphoreType.DMA((2,)),
            pltpu.SemaphoreType.DMA((2,)),
        ],
        compiler_params=pltpu.CompilerParams(
            collective_id=0, has_side_effects=True, vmem_limit_bytes=40 * 1024 * 1024
        ),
    )(
        *(
            pltpu.with_memory_space_constraint(operand, pltpu.HBM)
            for operand in (
                krylov_block, blade_class, neighbors, iface_rows, face_rows, stiffness, lumped_mass,
                precond, jnp.asarray(kron_table()),
            )
        )
    )


def solution(mesh):
    return jax.shard_map(
        on_device,
        mesh=mesh,
        in_specs=(
            P(None, "wheel", None, None, "slab"),
            P("wheel"),
            P(None, "slab"),
            P(None, "slab"),
            P(None, "slab"),
            P(None, None, None, "slab"),
            P(None, "slab"),
            P("wheel", "slab", None, None),
        ),
        out_specs=P("wheel", "slab", None, None),
        check_vma=False,
    )
```

```python
import math

import jax
import jax.numpy as jnp
import numpy as np
from jax import lax
from jax.experimental import pallas as pl
from jax.experimental.pallas import tpu as pltpu
from jax.sharding import PartitionSpec as P

import ml_dtypes

damping_ratio = 0.5
gyro_rate = 0.8
shift_value = 0.3
class_step = 0.125

SECT = 64
WHEEL = 32
SLAB = 8
MESH = pl.DeviceIdType.MESH
BF = jnp.bfloat16
F32 = jnp.float32


def slot_of(w):
    return (w // 8 % 2) * 16 + (w // 16) * 8 + w % 8


def worker_of(t, g):
    return (g // 4) * 16 + (g % 4) * 2 + t


def basis_table():
    b = np.arange(SECT)[:, None]
    s = np.arange(SECT)[None, :]
    p, q = b // 2, b % 2
    angle = 2.0 * math.pi / SECT * ((p * s) % SECT)
    inner = np.where(q == 0, np.cos(angle), np.sin(angle)) * math.sqrt(2.0 / SECT)
    edge = np.where(q == 0, 1.0, 1.0 - 2.0 * (s % 2)) * math.sqrt(1.0 / SECT)
    return np.where(p == 0, edge, inner).astype(np.float32)


def kron_table():
    sectors = [2 * w + part for w in sorted(range(WHEEL), key=slot_of) for part in range(2)]
    full = np.kron(basis_table()[:, sectors], np.eye(8, dtype=np.float32))
    high = full.astype(ml_dtypes.bfloat16)
    low = (full - high.astype(np.float32)).astype(ml_dtypes.bfloat16)
    return np.stack((high, low))


def one_hot(rows, cols, index_row):
    at = lax.broadcasted_iota(jnp.int32, (rows, cols), 0)
    return jnp.where(at == index_row, 1.0, 0.0).astype(BF)


def kernel(
    kb_hbm, bc_hbm, nb_hbm, ifr_hbm, fcr_hbm, st_hbm, ms_hbm, pc_hbm, km_hbm, out,
    kb, bc, nb, ifr, fcr, st, ms, pcv, kmv, hs, hsw, hr, hrw, sb, rv1, acc, sb2, rv2, hot, base, flip, pick_hot,
    ready, lsem, hsend, hrecv, ssem1, rsem1, ssem2, rsem2,
):
    w = lax.axis_index("wheel")
    j = lax.axis_index("slab")

    up = lax.rem(j + 1, SLAB)
    down = lax.rem(j + SLAB - 1, SLAB)
    nxt = lax.rem(w + 1, WHEEL)
    prv = lax.rem(w + WHEEL - 1, WHEEL)
    loads = [
        pltpu.make_async_copy(src, dst, lsem.at[n])
        for n, (src, dst) in enumerate(
            (
                (ifr_hbm, ifr), (fcr_hbm, fcr),
                *((kb_hbm.at[t, p], kb.at[t, p]) for p in range(2) for t in range(2)),
                (nb_hbm, nb), (st_hbm, st), (ms_hbm, ms), (bc_hbm, bc), (km_hbm, kmv), (pc_hbm, pcv),
            )
        )
    ]
    for load in loads:
        load.start()

    barrier = pltpu.get_barrier_semaphore()
    has_up = j < SLAB - 1
    has_down = j > 0

    def greet(to):
        pl.semaphore_signal(barrier, inc=1, device_id=to, device_id_type=MESH)

    @pl.when(has_up)
    def _():
        greet({"slab": up})

    @pl.when(has_down)
    def _():
        greet({"slab": down})

    greet({"wheel": nxt})
    greet({"wheel": prv})

    my_t = lax.rem(w, 2)
    along = lax.rem(w // 2, 8)
    my_g = (w // 16) * 4 + along
    works = along < 4

    late = jnp.logical_not(works)

    @pl.when(works)
    def _():
        mine = (w // 16) * 8 + lax.rem(w, 8)

        @pl.loop(1, 16)
        def _(i):
            other = lax.rem(mine + i, 16)
            greet({"wheel": (other // 8) * 16 + lax.rem(other, 8)})

    @pl.when(late)
    def _():
        greet({"wheel": w - 2 * jnp.where(along == 7, 7, along - 3)})

    for load in loads[:2]:
        load.wait()
    none = jnp.full((1, 64), -1, jnp.int32)
    index = jnp.concatenate(
        (ifr[1:2, :], none, none, ifr[0:1, :], fcr[1:2, :], none, none, fcr[0:1, :]), axis=1
    )
    pick_hot[...] = one_hot(256, 512, index)
    for load in loads[2:6]:
        load.wait()
    u = kb[0]
    v = kb[1]
    e = (u + damping_ratio * v).reshape(96, 256)
    ehi = e.astype(BF)
    elo = (e - ehi.astype(F32)).astype(BF)

    picks = jnp.dot(ehi, pick_hot[...], preferred_element_type=F32)
    hs[0] = (picks[0:48, 0:128] + pltpu.roll(picks[48:96, 0:128], 64, 1)).astype(BF)
    hs[1] = (pltpu.roll(picks[0:48, 128:256], 64, 1) + picks[48:96, 128:256]).astype(BF)
    hsw[0] = picks[48:96, 256:384].astype(BF)
    hsw[1] = picks[0:48, 384:512].astype(BF)

    greeted = 15 + jnp.where(along == 3, 3, 0) + jnp.where(along == 0, 1, 0)
    pl.semaphore_wait(
        barrier,
        2 + jnp.where(has_up, 1, 0) + jnp.where(has_down, 1, 0) + jnp.where(works, greeted, 0),
    )

    def tell(to):
        pl.semaphore_signal(ready, inc=1, device_id={"wheel": to}, device_id_type=MESH)

    @pl.when(along == 3)
    def _():
        for step in (2, 4, 6):
            tell(w + step)

    @pl.when(along == 0)
    def _():
        tell(w + 14)

    halos = [
        pltpu.make_async_remote_copy(
            src_ref=src, dst_ref=dst, send_sem=hsend.at[n], recv_sem=hrecv.at[n],
            device_id=to, device_id_type=MESH,
        )
        for n, (src, dst, to) in enumerate(
            (
                (hs.at[0], hr.at[0], {"slab": up}),
                (hs.at[1], hr.at[1], {"slab": down}),
                (hsw.at[0], hrw.at[0], {"wheel": nxt}),
                (hsw.at[1], hrw.at[1], {"wheel": prv}),
            )
        )
    ]

    @pl.when(has_up)
    def _():
        halos[0].start()

    @pl.when(has_down)
    def _():
        halos[1].start()

    halos[2].start()
    halos[3].start()

    lane = lax.broadcasted_iota(jnp.int32, (32, 128), 1)
    spot = lane // 32

    def squeeze(a, b, c, d, spare):
        turned = [pltpu.roll(d, shift, d.ndim - 1) for shift in (96, 64, 32)]
        return jnp.concatenate(
            [jnp.where(spare, x, y) for x, y in zip(turned, (a, b, c))], axis=-2
        )

    def fourth(a, b, c, place, first):
        axis = a.ndim - 1
        return jnp.where(
            place == first,
            pltpu.roll(a, 32, axis),
            jnp.where(place == lax.rem(first + 1, 4), pltpu.roll(b, 64, axis), pltpu.roll(c, 96, axis)),
        )

    def pack(t, res):
        for h in range(2):
            part = [res[:, c, :, h * 128 : (h + 1) * 128].reshape(32, 128) for c in range(3)]
            one = pltpu.roll(part[1], 32, 1)
            two = pltpu.roll(part[2], 64, 1)
            for g in range(4):
                tile = jnp.where(
                    spot == (g + 1) % 4, one, jnp.where(spot == (g + 2) % 4, two, part[0])
                )
                sb[t, h * 4 + g] = squeeze(
                    tile[0:8], tile[16:24], tile[8:16], tile[24:32], spot[:8] == (g + 3) % 4
                ).astype(BF)

    slot = lax.rem(w // 8, 2) * 16 + (w // 16) * 8 + lax.rem(w, 8)
    half_sem = rsem1.at[lax.rem(w // 8, 2)]

    def send(t):
        for n in range(8):
            g = lax.rem(n + 4 * (1 - w // 16), 8)
            to = (g // 4) * 16 + (n % 4) * 2 + t

            @pl.when(w != to)
            def _():
                pltpu.make_async_remote_copy(
                    src_ref=sb.at[t, g], dst_ref=rv1.at[slot], send_sem=ssem1, recv_sem=half_sem,
                    device_id={"wheel": to}, device_id_type=MESH,
                ).start()

            @pl.when(w == to)
            def _():
                pltpu.make_async_copy(sb.at[t, g], rv1.at[slot], half_sem).start()

    pack(0, v - shift_value * u)

    @pl.when(works)
    def _():
        send(0)

    def stencil(ke, k, picked):
        picked = picked.reshape(2, 3, 16, 256)
        for c in range(3):
            for d in range(3):
                ke[c] = ke[c] + st[c, d, k : k + 1, :] * picked[:, d]
        return ke

    for load in loads[6:10]:
        load.wait()
    own = jnp.concatenate((ehi, elo), axis=0)
    ke = [jnp.zeros((2, 16, 256), F32) for _ in range(3)]
    for k in range(8):
        both = jnp.dot(own, one_hot(256, 256, nb[k : k + 1, :]), preferred_element_type=F32)
        ke = stencil(ke, k, both[:96] + both[96:])

    for k in range(8):
        hot[k] = one_hot(256, 256, nb[k : k + 1, :] - 256)
    mass = [ms[c : c + 1, :] for c in range(3)]
    gyro = (-(mass[0] * v[:, 1]), mass[1] * v[:, 0], None)
    scale = [1.0 + class_step * bc[s].astype(F32) for s in range(2)]

    def scaled(part):
        return jnp.stack([scale[s] * part[s] for s in range(2)], axis=0)

    for c in range(3):
        row = -scaled(ke[c]) - shift_value * (mass[c] * v[:, c])
        if c < 2:
            row = row - gyro_rate * gyro[c]
        base[c] = row

    @pl.when(late)
    def _():
        pl.semaphore_wait(ready, 1)
        send(0)

    @pl.when(has_up)
    def _():
        halos[0].wait_send()
        halos[1].wait_recv()

    @pl.when(jnp.logical_not(has_up))
    def _():
        hr[1] = jnp.zeros((48, 128), BF)

    @pl.when(has_down)
    def _():
        halos[1].wait_send()
        halos[0].wait_recv()

    @pl.when(jnp.logical_not(has_down))
    def _():
        hr[0] = jnp.zeros((48, 128), BF)

    halos[2].wait()
    halos[3].wait()
    lower, upper = hr[0].astype(F32), hr[1].astype(F32)
    left_half = lax.broadcasted_iota(jnp.int32, (48, 128), 1) < 64
    iface = jnp.concatenate(
        (
            jnp.where(left_half, lower, pltpu.roll(upper, 64, 1)),
            jnp.where(left_half, pltpu.roll(lower, 64, 1), upper),
        ),
        axis=0,
    )
    face = jnp.concatenate(
        (
            hrw[0].astype(F32) + picks[48:96, 384:512],
            hrw[1].astype(F32) + picks[0:48, 256:384],
        ),
        axis=0,
    )
    halo = jnp.concatenate((iface, face), axis=1).astype(BF)
    ke = [jnp.zeros((2, 16, 256), F32) for _ in range(3)]
    for k in range(8):
        ke = stencil(ke, k, jnp.dot(halo, hot[k], preferred_element_type=F32))
    rows = [base[c] - scaled(ke[c]) for c in range(3)]
    pack(1, jnp.stack(rows, axis=1))
    send(1)

    loads[11].wait()
    for g in range(8):
        turned = pcv[0, g].T
        for n, part in enumerate((0, 2, 1, 3)):
            flip[g, n * 96 : n * 96 + 96] = turned[part * 96 : part * 96 + 96]

    def sent(count, sem):
        whole = rv1.at[pl.ds(0, count)]
        pltpu.make_async_copy(whole, whole, sem).wait()

    @pl.when(works)
    def _():
        loads[10].wait()

        corner = lax.rem(my_g, 4)
        place = lax.broadcasted_iota(jnp.int32, (16, 8, 128), 2) // 32

        def field(part):
            got = rv1[part * 16 : part * 16 + 16].astype(F32)
            a, b, c = (got[:, n * 8 : n * 8 + 8] for n in range(3))
            d = fourth(a, b, c, place, corner)
            return jnp.concatenate(
                [
                    jnp.concatenate(pair, axis=1).astype(BF).reshape(256, 128)
                    for pair in ((a, b), (c, d))
                ],
                axis=1,
            )

        def transform(first, part, data):
            rows = slice(first * 256, first * 256 + 256)
            cols = slice(part * 256, part * 256 + 256)
            return jnp.dot(kmv[0, rows, cols], data, preferred_element_type=F32) + jnp.dot(
                kmv[1, rows, cols], data, preferred_element_type=F32
            )

        def arrived(part):
            whole = rv1.at[pl.ds(part * 16, 16)]
            pltpu.make_async_copy(whole, whole, rsem1.at[part]).wait()

        def answer(to, group):
            @pl.when(w != to)
            def _():
                pltpu.make_async_remote_copy(
                    src_ref=sb2.at[to], dst_ref=rv2.at[my_t, my_g], send_sem=ssem2.at[group],
                    recv_sem=rsem2.at[my_t], device_id={"wheel": to}, device_id_type=MESH,
                ).start()

            @pl.when(w == to)
            def _():
                pltpu.make_async_copy(sb2.at[to], rv2.at[my_t, my_g], rsem2.at[my_t]).start()

        arrived(0)
        near = field(0)
        for first in range(2):
            acc[first] = transform(first, 0, near)
        arrived(1)
        far = field(1)
        for first in range(2):
            har = (acc[first] + transform(first, 1, far)).reshape(16, 2, 8, 256)
            sb2[first * 16 : first * 16 + 16] = squeeze(
                har[:, 0, :, :128], har[:, 0, :, 128:], har[:, 1, :, :128], har[:, 1, :, 128:],
                place == lax.rem(corner + 3, 4),
            ).astype(BF)
            for z in (0, 1, 2, 3):
                for core in range(2):
                    answer(first * 16 + z * 2 + core, 0)

        sent(15, ssem2.at[0])
        for first in range(2):
            for z in (6, 5, 7, 4):
                for core in range(2):
                    answer(first * 16 + z * 2 + core, 1)

    lane16 = lax.broadcasted_iota(jnp.int32, (16, 128), 1)

    def placed(t, g, q, at):
        shift = (at - 32 * (g % 4)) % 128
        got = rv2[t, g].astype(F32)
        if q == 0:
            x = got[:16]
        else:
            last = fourth(got[:8], got[8:16], got[16:], lane16[:8] // 32, g % 4)
            x = jnp.concatenate((got[16:], last), axis=0)
        return pltpu.roll(x, shift, 1) if shift else x

    def product(t, g):
        top = placed(t, g, 1, 96)
        lhs = jnp.concatenate(
            (jnp.where(lane16 < 96, placed(t, g, 0, 0), top), top), axis=1
        ).astype(BF)
        return jnp.dot(
            lhs[:, :192], flip[g, t * 192 : t * 192 + 192], preferred_element_type=F32
        )

    pltpu.make_async_copy(rv2.at[0], rv2.at[0], rsem2.at[0]).wait()
    for g in range(8):
        out[0, g] = product(0, g)

    pltpu.make_async_copy(rv2.at[1], rv2.at[1], rsem2.at[1]).wait()
    for g in range(8):
        out[0, g] += product(1, g)

    @pl.when(works)
    def _():
        sent(15, ssem1)
        sent(16, ssem2.at[1])

    @pl.when(late)
    def _():
        loads[10].wait()
        sent(16, ssem1)


def on_device(
    krylov_block, blade_class, neighbors, iface_rows, face_rows, stiffness, lumped_mass, precond
):
    vmem = pl.BlockSpec(memory_space=pltpu.VMEM)
    hbm = pl.BlockSpec(memory_space=pltpu.HBM)
    return pl.pallas_call(
        kernel,
        out_shape=jax.ShapeDtypeStruct((1, 8, 16, 384), F32),
        in_specs=[hbm] * 9,
        out_specs=vmem,
        scratch_shapes=[
            pltpu.VMEM((2, 2, 3, 16, 256), F32),
            pltpu.SMEM((2,), jnp.int32),
            pltpu.VMEM((8, 256), jnp.int32),
            pltpu.VMEM((2, 64), jnp.int32),
            pltpu.VMEM((2, 64), jnp.int32),
            pltpu.VMEM((3, 3, 8, 256), F32),
            pltpu.VMEM((3, 256), F32),
            pltpu.VMEM((1, 8, 384, 384), BF),
            pltpu.VMEM((2, 512, 512), BF),
            pltpu.VMEM((2, 48, 128), BF),
            pltpu.VMEM((2, 48, 128), BF),
            pltpu.VMEM((2, 48, 128), BF),
            pltpu.VMEM((2, 48, 128), BF),
            pltpu.VMEM((2, 8, 24, 128), BF),
            pltpu.VMEM((32, 24, 128), BF),
            pltpu.VMEM((2, 256, 256), F32),
            pltpu.VMEM((32, 24, 128), BF),
            pltpu.VMEM((2, 8, 24, 128), BF),
            pltpu.VMEM((8, 256, 256), BF),
            pltpu.VMEM((3, 2, 16, 256), F32),
            pltpu.VMEM((8, 384, 384), BF),
            pltpu.VMEM((256, 512), BF),
            pltpu.SemaphoreType.REGULAR,
            pltpu.SemaphoreType.DMA((12,)),
            pltpu.SemaphoreType.DMA((4,)),
            pltpu.SemaphoreType.DMA((4,)),
            pltpu.SemaphoreType.DMA,
            pltpu.SemaphoreType.DMA((2,)),
            pltpu.SemaphoreType.DMA((2,)),
            pltpu.SemaphoreType.DMA((2,)),
        ],
        compiler_params=pltpu.CompilerParams(
            collective_id=0, has_side_effects=True, vmem_limit_bytes=40 * 1024 * 1024
        ),
    )(
        *(
            pltpu.with_memory_space_constraint(operand, pltpu.HBM)
            for operand in (
                krylov_block, blade_class, neighbors, iface_rows, face_rows, stiffness, lumped_mass,
                precond, jnp.asarray(kron_table()),
            )
        )
    )


def solution(mesh):
    return jax.shard_map(
        on_device,
        mesh=mesh,
        in_specs=(
            P(None, "wheel", None, None, "slab"),
            P("wheel"),
            P(None, "slab"),
            P(None, "slab"),
            P(None, "slab"),
            P(None, None, None, "slab"),
            P(None, "slab"),
            P("wheel", "slab", None, None),
        ),
        out_specs=P("wheel", "slab", None, None),
        check_vma=False,
    )
```

```python
import math

import jax
import jax.numpy as jnp
import numpy as np
from jax import lax
from jax.experimental import pallas as pl
from jax.experimental.pallas import tpu as pltpu
from jax.sharding import PartitionSpec as P

import ml_dtypes

damping_ratio = 0.5
gyro_rate = 0.8
shift_value = 0.3
class_step = 0.125

SECT = 64
WHEEL = 32
SLAB = 8
MESH = pl.DeviceIdType.MESH
BF = jnp.bfloat16
F32 = jnp.float32


def slot_of(w):
    return (w // 8 % 2) * 16 + (w // 16) * 8 + w % 8


def worker_of(t, g):
    return (g // 4) * 16 + (g % 4) * 2 + t


def basis_table():
    b = np.arange(SECT)[:, None]
    s = np.arange(SECT)[None, :]
    p, q = b // 2, b % 2
    angle = 2.0 * math.pi / SECT * ((p * s) % SECT)
    inner = np.where(q == 0, np.cos(angle), np.sin(angle)) * math.sqrt(2.0 / SECT)
    edge = np.where(q == 0, 1.0, 1.0 - 2.0 * (s % 2)) * math.sqrt(1.0 / SECT)
    return np.where(p == 0, edge, inner).astype(np.float32)


def kron_table():
    sectors = [2 * w + part for w in sorted(range(WHEEL), key=slot_of) for part in range(2)]
    full = np.kron(basis_table()[:, sectors], np.eye(8, dtype=np.float32))
    high = full.astype(ml_dtypes.bfloat16)
    low = (full - high.astype(np.float32)).astype(ml_dtypes.bfloat16)
    return np.stack((high, low))


def one_hot(rows, cols, index_row):
    at = lax.broadcasted_iota(jnp.int32, (rows, cols), 0)
    return jnp.where(at == index_row, 1.0, 0.0).astype(BF)


def kernel(
    kb_hbm, bc_hbm, nb_hbm, ifr_hbm, fcr_hbm, st_hbm, ms_hbm, pc_hbm, km_hbm, out,
    kb, bc, nb, ifr, fcr, st, ms, pcv, kmv, hs, hsw, hr, hrw, sb, rv1, acc, sb2, rv2, hot, base, flip, pick_hot,
    ready, lsem, hsend, hrecv, ssem1, rsem1, ssem2, rsem2,
):
    w = lax.axis_index("wheel")
    j = lax.axis_index("slab")

    up = lax.rem(j + 1, SLAB)
    down = lax.rem(j + SLAB - 1, SLAB)
    nxt = lax.rem(w + 1, WHEEL)
    prv = lax.rem(w + WHEEL - 1, WHEEL)
    loads = [
        pltpu.make_async_copy(src, dst, lsem.at[n])
        for n, (src, dst) in enumerate(
            (
                (ifr_hbm, ifr), (fcr_hbm, fcr),
                *((kb_hbm.at[t, p], kb.at[t, p]) for p in range(2) for t in range(2)),
                (nb_hbm, nb), (st_hbm, st), (ms_hbm, ms), (bc_hbm, bc), (km_hbm, kmv), (pc_hbm, pcv),
            )
        )
    ]
    for load in loads:
        load.start()

    barrier = pltpu.get_barrier_semaphore()
    has_up = j < SLAB - 1
    has_down = j > 0

    def greet(to):
        pl.semaphore_signal(barrier, inc=1, device_id=to, device_id_type=MESH)

    @pl.when(has_up)
    def _():
        greet({"slab": up})

    @pl.when(has_down)
    def _():
        greet({"slab": down})

    greet({"wheel": nxt})
    greet({"wheel": prv})

    my_t = lax.rem(w, 2)
    along = lax.rem(w // 2, 8)
    my_g = (w // 16) * 4 + along
    works = along < 4

    late = jnp.logical_not(works)
    side = (w < 16)
    relayed = late & side
    direct = late & jnp.logical_not(side)

    @pl.when(works)
    def _():
        mine = (w // 16) * 8 + lax.rem(w, 8)

        @pl.loop(1, 16)
        def _(i):
            other = lax.rem(mine + i, 16)
            greet({"wheel": (other // 8) * 16 + lax.rem(other, 8)})

        @pl.loop(0, 8)
        def _(i):
            greet({"wheel": 24 + i})

    @pl.when(relayed)
    def _():
        greet({"wheel": w - 2 * jnp.where(along == 7, 7, along - 3)})

    for load in loads[:2]:
        load.wait()
    none = jnp.full((1, 64), -1, jnp.int32)
    index = jnp.concatenate(
        (ifr[1:2, :], none, none, ifr[0:1, :], fcr[1:2, :], none, none, fcr[0:1, :]), axis=1
    )
    pick_hot[...] = one_hot(256, 512, index)
    for load in loads[2:6]:
        load.wait()
    u = kb[0]
    v = kb[1]
    e = (u + damping_ratio * v).reshape(96, 256)
    ehi = e.astype(BF)

    picks = jnp.dot(ehi, pick_hot[...], preferred_element_type=F32)
    hs[0] = (picks[0:48, 0:128] + pltpu.roll(picks[48:96, 0:128], 64, 1)).astype(BF)
    hs[1] = (pltpu.roll(picks[0:48, 128:256], 64, 1) + picks[48:96, 128:256]).astype(BF)
    hsw[0] = picks[48:96, 256:384].astype(BF)
    hsw[1] = picks[0:48, 384:512].astype(BF)

    told = jnp.where(along == 3, 3, 0) + jnp.where(along == 0, 1, 0)
    greeted = jnp.where(works, 15 + jnp.where(side, told, 0), jnp.where(direct, 16, 0))
    pl.semaphore_wait(
        barrier, 2 + jnp.where(has_up, 1, 0) + jnp.where(has_down, 1, 0) + greeted
    )

    def tell(to):
        pl.semaphore_signal(ready, inc=1, device_id={"wheel": to}, device_id_type=MESH)

    @pl.when(side & (along == 3))
    def _():
        for step in (2, 4, 6):
            tell(w + step)

    @pl.when(side & (along == 0))
    def _():
        tell(w + 14)

    halos = [
        pltpu.make_async_remote_copy(
            src_ref=src, dst_ref=dst, send_sem=hsend.at[n], recv_sem=hrecv.at[n],
            device_id=to, device_id_type=MESH,
        )
        for n, (src, dst, to) in enumerate(
            (
                (hs.at[0], hr.at[0], {"slab": up}),
                (hs.at[1], hr.at[1], {"slab": down}),
                (hsw.at[0], hrw.at[0], {"wheel": nxt}),
                (hsw.at[1], hrw.at[1], {"wheel": prv}),
            )
        )
    ]

    @pl.when(has_up)
    def _():
        halos[0].start()

    @pl.when(has_down)
    def _():
        halos[1].start()

    halos[2].start()
    halos[3].start()

    lane = lax.broadcasted_iota(jnp.int32, (32, 128), 1)
    spot = lane // 32

    def squeeze(a, b, c, d, spare):
        turned = [pltpu.roll(d, shift, d.ndim - 1) for shift in (96, 64, 32)]
        return jnp.concatenate(
            [jnp.where(spare, x, y) for x, y in zip(turned, (a, b, c))], axis=-2
        )

    def fourth(a, b, c, place, first):
        axis = a.ndim - 1
        return jnp.where(
            place == first,
            pltpu.roll(a, 32, axis),
            jnp.where(place == lax.rem(first + 1, 4), pltpu.roll(b, 64, axis), pltpu.roll(c, 96, axis)),
        )

    def pack(t, res):
        for h in range(2):
            part = [res[:, c, :, h * 128 : (h + 1) * 128].reshape(32, 128) for c in range(3)]
            one = pltpu.roll(part[1], 32, 1)
            two = pltpu.roll(part[2], 64, 1)
            for g in range(4):
                tile = jnp.where(
                    spot == (g + 1) % 4, one, jnp.where(spot == (g + 2) % 4, two, part[0])
                )
                sb[t, h * 4 + g] = squeeze(
                    tile[0:8], tile[16:24], tile[8:16], tile[24:32], spot[:8] == (g + 3) % 4
                ).astype(BF)

    slot = lax.rem(w // 8, 2) * 16 + (w // 16) * 8 + lax.rem(w, 8)
    half_sem = rsem1.at[lax.rem(w // 8, 2)]

    def send(t):
        for n in range(8):
            g = lax.rem(n + 4 * (1 - w // 16), 8)
            to = (g // 4) * 16 + (n % 4) * 2 + t

            @pl.when(w != to)
            def _():
                pltpu.make_async_remote_copy(
                    src_ref=sb.at[t, g], dst_ref=rv1.at[slot], send_sem=ssem1, recv_sem=half_sem,
                    device_id={"wheel": to}, device_id_type=MESH,
                ).start()

            @pl.when(w == to)
            def _():
                pltpu.make_async_copy(sb.at[t, g], rv1.at[slot], half_sem).start()

    pack(0, v - shift_value * u)

    @pl.when(works | direct)
    def _():
        send(0)

    def stencil(ke, k, picked):
        picked = picked.reshape(2, 3, 16, 256)
        for c in range(3):
            for d in range(3):
                ke[c] = ke[c] + st[c, d, k : k + 1, :] * picked[:, d]
        return ke

    for load in loads[6:10]:
        load.wait()
    elo = (e - ehi.astype(F32)).astype(BF)
    own = jnp.concatenate((ehi, elo), axis=0)
    ke = [jnp.zeros((2, 16, 256), F32) for _ in range(3)]
    for k in range(8):
        both = jnp.dot(own, one_hot(256, 256, nb[k : k + 1, :]), preferred_element_type=F32)
        ke = stencil(ke, k, both[:96] + both[96:])

    for k in range(8):
        hot[k] = one_hot(256, 256, nb[k : k + 1, :] - 256)
    mass = [ms[c : c + 1, :] for c in range(3)]
    gyro = (-(mass[0] * v[:, 1]), mass[1] * v[:, 0], None)
    scale = [1.0 + class_step * bc[s].astype(F32) for s in range(2)]

    def scaled(part):
        return jnp.stack([scale[s] * part[s] for s in range(2)], axis=0)

    for c in range(3):
        row = -scaled(ke[c]) - shift_value * (mass[c] * v[:, c])
        if c < 2:
            row = row - gyro_rate * gyro[c]
        base[c] = row

    @pl.when(relayed)
    def _():
        pl.semaphore_wait(ready, 1)
        send(0)

    @pl.when(has_up)
    def _():
        halos[0].wait_send()
        halos[1].wait_recv()

    @pl.when(jnp.logical_not(has_up))
    def _():
        hr[1] = jnp.zeros((48, 128), BF)

    @pl.when(has_down)
    def _():
        halos[1].wait_send()
        halos[0].wait_recv()

    @pl.when(jnp.logical_not(has_down))
    def _():
        hr[0] = jnp.zeros((48, 128), BF)

    halos[2].wait()
    halos[3].wait()
    lower, upper = hr[0].astype(F32), hr[1].astype(F32)
    left_half = lax.broadcasted_iota(jnp.int32, (48, 128), 1) < 64
    iface = jnp.concatenate(
        (
            jnp.where(left_half, lower, pltpu.roll(upper, 64, 1)),
            jnp.where(left_half, pltpu.roll(lower, 64, 1), upper),
        ),
        axis=0,
    )
    face = jnp.concatenate(
        (
            hrw[0].astype(F32) + picks[48:96, 384:512],
            hrw[1].astype(F32) + picks[0:48, 256:384],
        ),
        axis=0,
    )
    halo = jnp.concatenate((iface, face), axis=1).astype(BF)
    ke = [jnp.zeros((2, 16, 256), F32) for _ in range(3)]
    for k in range(8):
        ke = stencil(ke, k, jnp.dot(halo, hot[k], preferred_element_type=F32))
    rows = [base[c] - scaled(ke[c]) for c in range(3)]
    pack(1, jnp.stack(rows, axis=1))
    send(1)

    loads[11].wait()
    for g in range(8):
        turned = pcv[0, g].T
        for n, part in enumerate((0, 2, 1, 3)):
            flip[g, n * 96 : n * 96 + 96] = turned[part * 96 : part * 96 + 96]

    def sent(count, sem):
        whole = rv1.at[pl.ds(0, count)]
        pltpu.make_async_copy(whole, whole, sem).wait()

    @pl.when(works)
    def _():
        loads[10].wait()

        corner = lax.rem(my_g, 4)
        place = lax.broadcasted_iota(jnp.int32, (16, 8, 128), 2) // 32

        def field(part):
            got = rv1[part * 16 : part * 16 + 16].astype(F32)
            a, b, c = (got[:, n * 8 : n * 8 + 8] for n in range(3))
            d = fourth(a, b, c, place, corner)
            return jnp.concatenate(
                [
                    jnp.concatenate(pair, axis=1).astype(BF).reshape(256, 128)
                    for pair in ((a, b), (c, d))
                ],
                axis=1,
            )

        def transform(first, part, data):
            rows = slice(first * 256, first * 256 + 256)
            cols = slice(part * 256, part * 256 + 256)
            return jnp.dot(kmv[0, rows, cols], data, preferred_element_type=F32) + jnp.dot(
                kmv[1, rows, cols], data, preferred_element_type=F32
            )

        def arrived(part):
            whole = rv1.at[pl.ds(part * 16, 16)]
            pltpu.make_async_copy(whole, whole, rsem1.at[part]).wait()

        def answer(to, group):
            @pl.when(w != to)
            def _():
                pltpu.make_async_remote_copy(
                    src_ref=sb2.at[to], dst_ref=rv2.at[my_t, my_g], send_sem=ssem2.at[group],
                    recv_sem=rsem2.at[my_t], device_id={"wheel": to}, device_id_type=MESH,
                ).start()

            @pl.when(w == to)
            def _():
                pltpu.make_async_copy(sb2.at[to], rv2.at[my_t, my_g], rsem2.at[my_t]).start()

        arrived(0)
        near = field(0)
        for first in range(2):
            acc[first] = transform(first, 0, near)
        arrived(1)
        far = field(1)
        for first in range(2):
            har = (acc[first] + transform(first, 1, far)).reshape(16, 2, 8, 256)
            sb2[first * 16 : first * 16 + 16] = squeeze(
                har[:, 0, :, :128], har[:, 0, :, 128:], har[:, 1, :, :128], har[:, 1, :, 128:],
                place == lax.rem(corner + 3, 4),
            ).astype(BF)
            for z in (0, 1, 2, 3):
                for core in range(2):
                    answer(first * 16 + z * 2 + core, 0)

        sent(15, ssem2.at[0])
        for first in range(2):
            for z in (6, 5, 7, 4):
                for core in range(2):
                    answer(first * 16 + z * 2 + core, 1)

    lane16 = lax.broadcasted_iota(jnp.int32, (16, 128), 1)

    def placed(t, g, q, at):
        shift = (at - 32 * (g % 4)) % 128
        got = rv2[t, g].astype(F32)
        if q == 0:
            x = got[:16]
        else:
            last = fourth(got[:8], got[8:16], got[16:], lane16[:8] // 32, g % 4)
            x = jnp.concatenate((got[16:], last), axis=0)
        return pltpu.roll(x, shift, 1) if shift else x

    def product(t, g):
        top = placed(t, g, 1, 96)
        lhs = jnp.concatenate(
            (jnp.where(lane16 < 96, placed(t, g, 0, 0), top), top), axis=1
        ).astype(BF)
        return jnp.dot(
            lhs[:, :192], flip[g, t * 192 : t * 192 + 192], preferred_element_type=F32
        )

    pltpu.make_async_copy(rv2.at[0], rv2.at[0], rsem2.at[0]).wait()
    for g in range(8):
        out[0, g] = product(0, g)

    pltpu.make_async_copy(rv2.at[1], rv2.at[1], rsem2.at[1]).wait()
    for g in range(8):
        out[0, g] += product(1, g)

    @pl.when(works)
    def _():
        sent(15, ssem1)
        sent(16, ssem2.at[1])

    @pl.when(late)
    def _():
        loads[10].wait()
        sent(16, ssem1)


def on_device(
    krylov_block, blade_class, neighbors, iface_rows, face_rows, stiffness, lumped_mass, precond
):
    vmem = pl.BlockSpec(memory_space=pltpu.VMEM)
    hbm = pl.BlockSpec(memory_space=pltpu.HBM)
    return pl.pallas_call(
        kernel,
        out_shape=jax.ShapeDtypeStruct((1, 8, 16, 384), F32),
        in_specs=[hbm] * 9,
        out_specs=vmem,
        scratch_shapes=[
            pltpu.VMEM((2, 2, 3, 16, 256), F32),
            pltpu.SMEM((2,), jnp.int32),
            pltpu.VMEM((8, 256), jnp.int32),
            pltpu.VMEM((2, 64), jnp.int32),
            pltpu.VMEM((2, 64), jnp.int32),
            pltpu.VMEM((3, 3, 8, 256), F32),
            pltpu.VMEM((3, 256), F32),
            pltpu.VMEM((1, 8, 384, 384), BF),
            pltpu.VMEM((2, 512, 512), BF),
            pltpu.VMEM((2, 48, 128), BF),
            pltpu.VMEM((2, 48, 128), BF),
            pltpu.VMEM((2, 48, 128), BF),
            pltpu.VMEM((2, 48, 128), BF),
            pltpu.VMEM((2, 8, 24, 128), BF),
            pltpu.VMEM((32, 24, 128), BF),
            pltpu.VMEM((2, 256, 256), F32),
            pltpu.VMEM((32, 24, 128), BF),
            pltpu.VMEM((2, 8, 24, 128), BF),
            pltpu.VMEM((8, 256, 256), BF),
            pltpu.VMEM((3, 2, 16, 256), F32),
            pltpu.VMEM((8, 384, 384), BF),
            pltpu.VMEM((256, 512), BF),
            pltpu.SemaphoreType.REGULAR,
            pltpu.SemaphoreType.DMA((12,)),
            pltpu.SemaphoreType.DMA((4,)),
            pltpu.SemaphoreType.DMA((4,)),
            pltpu.SemaphoreType.DMA,
            pltpu.SemaphoreType.DMA((2,)),
            pltpu.SemaphoreType.DMA((2,)),
            pltpu.SemaphoreType.DMA((2,)),
        ],
        compiler_params=pltpu.CompilerParams(
            collective_id=0, has_side_effects=True, vmem_limit_bytes=40 * 1024 * 1024
        ),
    )(
        *(
            pltpu.with_memory_space_constraint(operand, pltpu.HBM)
            for operand in (
                krylov_block, blade_class, neighbors, iface_rows, face_rows, stiffness, lumped_mass,
                precond, jnp.asarray(kron_table()),
            )
        )
    )


def solution(mesh):
    return jax.shard_map(
        on_device,
        mesh=mesh,
        in_specs=(
            P(None, "wheel", None, None, "slab"),
            P("wheel"),
            P(None, "slab"),
            P(None, "slab"),
            P(None, "slab"),
            P(None, None, None, "slab"),
            P(None, "slab"),
            P("wheel", "slab", None, None),
        ),
        out_specs=P("wheel", "slab", None, None),
        check_vma=False,
    )
```

```python
import math

import jax
import jax.numpy as jnp
import numpy as np
from jax import lax
from jax.experimental import pallas as pl
from jax.experimental.pallas import tpu as pltpu
from jax.sharding import PartitionSpec as P

import ml_dtypes

damping_ratio = 0.5
gyro_rate = 0.8
shift_value = 0.3
class_step = 0.125

SECT = 64
WHEEL = 32
SLAB = 8
MESH = pl.DeviceIdType.MESH
BF = jnp.bfloat16
F32 = jnp.float32


def slot_of(w):
    return (w // 8 % 2) * 16 + (w // 16) * 8 + w % 8


def worker_of(t, g):
    return (g // 4) * 16 + (g % 4) * 2 + t


def basis_table():
    b = np.arange(SECT)[:, None]
    s = np.arange(SECT)[None, :]
    p, q = b // 2, b % 2
    angle = 2.0 * math.pi / SECT * ((p * s) % SECT)
    inner = np.where(q == 0, np.cos(angle), np.sin(angle)) * math.sqrt(2.0 / SECT)
    edge = np.where(q == 0, 1.0, 1.0 - 2.0 * (s % 2)) * math.sqrt(1.0 / SECT)
    return np.where(p == 0, edge, inner).astype(np.float32)


def kron_table():
    sectors = [2 * w + part for w in sorted(range(WHEEL), key=slot_of) for part in range(2)]
    full = np.kron(basis_table()[:, sectors], np.eye(8, dtype=np.float32))
    high = full.astype(ml_dtypes.bfloat16)
    low = (full - high.astype(np.float32)).astype(ml_dtypes.bfloat16)
    return np.stack((high, low))


def one_hot(rows, cols, index_row):
    at = lax.broadcasted_iota(jnp.int32, (rows, cols), 0)
    return jnp.where(at == index_row, 1.0, 0.0).astype(BF)


def kernel(
    kb_hbm, bc_hbm, nb_hbm, ifr_hbm, fcr_hbm, st_hbm, ms_hbm, pc_hbm, km_hbm, out,
    kb, bc, nb, ifr, fcr, st, ms, pcv, kmv, hs, hsw, hr, hrw, sb, rv1, acc, sb2, rv2, hot, base, flip, pick_hot,
    ready, lsem, hsend, hrecv, ssem1, rsem1, ssem2, rsem2,
):
    w = lax.axis_index("wheel")
    j = lax.axis_index("slab")

    up = lax.rem(j + 1, SLAB)
    down = lax.rem(j + SLAB - 1, SLAB)
    nxt = lax.rem(w + 1, WHEEL)
    prv = lax.rem(w + WHEEL - 1, WHEEL)
    loads = [
        pltpu.make_async_copy(src, dst, lsem.at[n])
        for n, (src, dst) in enumerate(
            (
                (ifr_hbm, ifr), (fcr_hbm, fcr),
                *((kb_hbm.at[t, p], kb.at[t, p]) for p in range(2) for t in range(2)),
                (nb_hbm, nb), (st_hbm, st), (ms_hbm, ms), (bc_hbm, bc), (km_hbm, kmv), (pc_hbm, pcv),
            )
        )
    ]
    for load in loads:
        load.start()

    barrier = pltpu.get_barrier_semaphore()
    has_up = j < SLAB - 1
    has_down = j > 0

    def greet(to):
        pl.semaphore_signal(barrier, inc=1, device_id=to, device_id_type=MESH)

    @pl.when(has_up)
    def _():
        greet({"slab": up})

    @pl.when(has_down)
    def _():
        greet({"slab": down})

    greet({"wheel": nxt})
    greet({"wheel": prv})

    my_t = lax.rem(w, 2)
    along = lax.rem(w // 2, 8)
    my_g = (w // 16) * 4 + along
    works = along < 4

    late = jnp.logical_not(works)
    side = (w < 16)
    relayed = late & side
    direct = late & jnp.logical_not(side)

    @pl.when(works)
    def _():
        mine = (w // 16) * 8 + lax.rem(w, 8)

        @pl.loop(1, 16)
        def _(i):
            other = lax.rem(mine + i, 16)
            greet({"wheel": (other // 8) * 16 + lax.rem(other, 8)})

        @pl.loop(0, 8)
        def _(i):
            greet({"wheel": 24 + i})

    @pl.when(relayed)
    def _():
        greet({"wheel": w - 2 * jnp.where(along == 7, 7, along - 3)})

    for load in loads[:2]:
        load.wait()
    none = jnp.full((1, 64), -1, jnp.int32)
    index = jnp.concatenate(
        (ifr[1:2, :], none, none, ifr[0:1, :], fcr[1:2, :], none, none, fcr[0:1, :]), axis=1
    )
    pick_hot[...] = one_hot(256, 512, index)
    for load in loads[2:6]:
        load.wait()
    u = kb[0]
    v = kb[1]
    e = (u + damping_ratio * v).reshape(96, 256)
    ehi = e.astype(BF)

    picks = jnp.dot(ehi, pick_hot[...], preferred_element_type=F32)
    hs[0] = (picks[0:48, 0:128] + pltpu.roll(picks[48:96, 0:128], 64, 1)).astype(BF)
    hs[1] = (pltpu.roll(picks[0:48, 128:256], 64, 1) + picks[48:96, 128:256]).astype(BF)
    hsw[0] = picks[48:96, 256:384].astype(BF)
    hsw[1] = picks[0:48, 384:512].astype(BF)

    told = jnp.where(along == 3, 3, 0) + jnp.where(along == 0, 1, 0)
    greeted = jnp.where(works, 15 + jnp.where(side, told, 0), jnp.where(direct, 16, 0))
    pl.semaphore_wait(
        barrier, 2 + jnp.where(has_up, 1, 0) + jnp.where(has_down, 1, 0) + greeted
    )

    def tell(to):
        pl.semaphore_signal(ready, inc=1, device_id={"wheel": to}, device_id_type=MESH)

    @pl.when(side & (along == 3))
    def _():
        for step in (2, 4, 6):
            tell(w + step)

    @pl.when(side & (along == 0))
    def _():
        tell(w + 14)

    halos = [
        pltpu.make_async_remote_copy(
            src_ref=src, dst_ref=dst, send_sem=hsend.at[n], recv_sem=hrecv.at[n],
            device_id=to, device_id_type=MESH,
        )
        for n, (src, dst, to) in enumerate(
            (
                (hs.at[0], hr.at[0], {"slab": up}),
                (hs.at[1], hr.at[1], {"slab": down}),
                (hsw.at[0], hrw.at[0], {"wheel": nxt}),
                (hsw.at[1], hrw.at[1], {"wheel": prv}),
            )
        )
    ]

    @pl.when(has_up)
    def _():
        halos[0].start()

    @pl.when(has_down)
    def _():
        halos[1].start()

    halos[2].start()
    halos[3].start()

    lane = lax.broadcasted_iota(jnp.int32, (32, 128), 1)
    spot = lane // 32

    def squeeze(a, b, c, d, spare):
        turned = [pltpu.roll(d, shift, d.ndim - 1) for shift in (96, 64, 32)]
        return jnp.concatenate(
            [jnp.where(spare, x, y) for x, y in zip(turned, (a, b, c))], axis=-2
        )

    def fourth(a, b, c, place, first):
        axis = a.ndim - 1
        return jnp.where(
            place == first,
            pltpu.roll(a, 32, axis),
            jnp.where(place == lax.rem(first + 1, 4), pltpu.roll(b, 64, axis), pltpu.roll(c, 96, axis)),
        )

    def pack(t, res):
        for h in range(2):
            part = [res[:, c, :, h * 128 : (h + 1) * 128].reshape(32, 128) for c in range(3)]
            one = pltpu.roll(part[1], 32, 1)
            two = pltpu.roll(part[2], 64, 1)
            for g in range(4):
                tile = jnp.where(
                    spot == (g + 1) % 4, one, jnp.where(spot == (g + 2) % 4, two, part[0])
                )
                sb[t, h * 4 + g] = squeeze(
                    tile[0:8], tile[16:24], tile[8:16], tile[24:32], spot[:8] == (g + 3) % 4
                ).astype(BF)

    slot = lax.rem(w // 8, 2) * 16 + (w // 16) * 8 + lax.rem(w, 8)
    half_sem = rsem1.at[lax.rem(w // 8, 2)]

    def send(t):
        for n in range(8):
            g = lax.rem(n + 4 * (1 - w // 16), 8)
            to = (g // 4) * 16 + (n % 4) * 2 + t

            @pl.when(w != to)
            def _():
                pltpu.make_async_remote_copy(
                    src_ref=sb.at[t, g], dst_ref=rv1.at[slot], send_sem=ssem1, recv_sem=half_sem,
                    device_id={"wheel": to}, device_id_type=MESH,
                ).start()

            @pl.when(w == to)
            def _():
                pltpu.make_async_copy(sb.at[t, g], rv1.at[slot], half_sem).start()

    pack(0, v - shift_value * u)

    @pl.when(works | direct)
    def _():
        send(0)

    def stencil(ke, k, picked):
        picked = picked.reshape(2, 3, 16, 256)
        for c in range(3):
            for d in range(3):
                ke[c] = ke[c] + st[c, d, k : k + 1, :] * picked[:, d]
        return ke

    for load in loads[6:10]:
        load.wait()
    elo = (e - ehi.astype(F32)).astype(BF)
    own = jnp.concatenate((ehi, elo), axis=0)
    ke = [jnp.zeros((2, 16, 256), F32) for _ in range(3)]
    for k in range(8):
        both = jnp.dot(own, one_hot(256, 256, nb[k : k + 1, :]), preferred_element_type=F32)
        ke = stencil(ke, k, both[:96] + both[96:])

    for k in range(8):
        hot[k] = one_hot(256, 256, nb[k : k + 1, :] - 256)
    mass = [ms[c : c + 1, :] for c in range(3)]
    gyro = (-(mass[0] * v[:, 1]), mass[1] * v[:, 0], None)
    scale = [1.0 + class_step * bc[s].astype(F32) for s in range(2)]

    def scaled(part):
        return jnp.stack([scale[s] * part[s] for s in range(2)], axis=0)

    for c in range(3):
        row = -scaled(ke[c]) - shift_value * (mass[c] * v[:, c])
        if c < 2:
            row = row - gyro_rate * gyro[c]
        base[c] = row

    @pl.when(relayed)
    def _():
        pl.semaphore_wait(ready, 1)
        send(0)

    @pl.when(has_up)
    def _():
        halos[0].wait_send()
        halos[1].wait_recv()

    @pl.when(jnp.logical_not(has_up))
    def _():
        hr[1] = jnp.zeros((48, 128), BF)

    @pl.when(has_down)
    def _():
        halos[1].wait_send()
        halos[0].wait_recv()

    @pl.when(jnp.logical_not(has_down))
    def _():
        hr[0] = jnp.zeros((48, 128), BF)

    halos[2].wait()
    halos[3].wait()
    lower, upper = hr[0].astype(F32), hr[1].astype(F32)
    left_half = lax.broadcasted_iota(jnp.int32, (48, 128), 1) < 64
    iface = jnp.concatenate(
        (
            jnp.where(left_half, lower, pltpu.roll(upper, 64, 1)),
            jnp.where(left_half, pltpu.roll(lower, 64, 1), upper),
        ),
        axis=0,
    )
    face = jnp.concatenate(
        (
            hrw[0].astype(F32) + picks[48:96, 384:512],
            hrw[1].astype(F32) + picks[0:48, 256:384],
        ),
        axis=0,
    )
    halo = jnp.concatenate((iface, face), axis=1).astype(BF)
    ke = [jnp.zeros((2, 16, 256), F32) for _ in range(3)]
    for k in range(8):
        ke = stencil(ke, k, jnp.dot(halo, hot[k], preferred_element_type=F32))
    rows = [base[c] - scaled(ke[c]) for c in range(3)]
    pack(1, jnp.stack(rows, axis=1))
    send(1)

    loads[11].wait()
    for g in range(8):
        turned = pcv[0, g].T
        for n, part in enumerate((0, 2, 1, 3)):
            flip[g, n * 96 : n * 96 + 96] = turned[part * 96 : part * 96 + 96]

    def sent(count, sem):
        whole = rv1.at[pl.ds(0, count)]
        pltpu.make_async_copy(whole, whole, sem).wait()

    @pl.when(works)
    def _():
        loads[10].wait()

        corner = lax.rem(my_g, 4)
        place = lax.broadcasted_iota(jnp.int32, (16, 8, 128), 2) // 32

        def field(part):
            got = rv1[part * 16 : part * 16 + 16].astype(F32)
            a, b, c = (got[:, n * 8 : n * 8 + 8] for n in range(3))
            d = fourth(a, b, c, place, corner)
            return jnp.concatenate(
                [
                    jnp.concatenate(pair, axis=1).astype(BF).reshape(256, 128)
                    for pair in ((a, b), (c, d))
                ],
                axis=1,
            )

        def transform(first, part, data):
            rows = slice(first * 256, first * 256 + 256)
            cols = slice(part * 256, part * 256 + 256)
            return jnp.dot(kmv[0, rows, cols], data, preferred_element_type=F32) + jnp.dot(
                kmv[1, rows, cols], data, preferred_element_type=F32
            )

        def arrived(part):
            whole = rv1.at[pl.ds(part * 16, 16)]
            pltpu.make_async_copy(whole, whole, rsem1.at[part]).wait()

        def answer(to, group):
            @pl.when(w != to)
            def _():
                pltpu.make_async_remote_copy(
                    src_ref=sb2.at[to], dst_ref=rv2.at[my_t, my_g], send_sem=ssem2.at[group],
                    recv_sem=rsem2.at[my_t], device_id={"wheel": to}, device_id_type=MESH,
                ).start()

            @pl.when(w == to)
            def _():
                pltpu.make_async_copy(sb2.at[to], rv2.at[my_t, my_g], rsem2.at[my_t]).start()

        arrived(0)
        near = field(0)
        for first in range(2):
            acc[first] = transform(first, 0, near)
        arrived(1)
        far = field(1)
        for first in range(2):
            har = (acc[first] + transform(first, 1, far)).reshape(16, 2, 8, 256)
            sb2[first * 16 : first * 16 + 16] = squeeze(
                har[:, 0, :, :128], har[:, 0, :, 128:], har[:, 1, :, :128], har[:, 1, :, 128:],
                place == lax.rem(corner + 3, 4),
            ).astype(BF)
            for z in (0, 1, 6, 2, 3):
                for core in range(2):
                    answer(first * 16 + z * 2 + core, 0)

        sent(19, ssem2.at[0])
        for first in range(2):
            for z in (5, 7, 4):
                for core in range(2):
                    answer(first * 16 + z * 2 + core, 1)

    lane16 = lax.broadcasted_iota(jnp.int32, (16, 128), 1)

    def placed(t, g, q, at):
        shift = (at - 32 * (g % 4)) % 128
        got = rv2[t, g].astype(F32)
        if q == 0:
            x = got[:16]
        else:
            last = fourth(got[:8], got[8:16], got[16:], lane16[:8] // 32, g % 4)
            x = jnp.concatenate((got[16:], last), axis=0)
        return pltpu.roll(x, shift, 1) if shift else x

    def product(t, g):
        top = placed(t, g, 1, 96)
        lhs = jnp.concatenate(
            (jnp.where(lane16 < 96, placed(t, g, 0, 0), top), top), axis=1
        ).astype(BF)
        return jnp.dot(
            lhs[:, :192], flip[g, t * 192 : t * 192 + 192], preferred_element_type=F32
        )

    pltpu.make_async_copy(rv2.at[0], rv2.at[0], rsem2.at[0]).wait()
    for g in range(8):
        out[0, g] = product(0, g)

    pltpu.make_async_copy(rv2.at[1], rv2.at[1], rsem2.at[1]).wait()
    for g in range(8):
        out[0, g] += product(1, g)

    @pl.when(works)
    def _():
        sent(15, ssem1)
        sent(12, ssem2.at[1])

    @pl.when(late)
    def _():
        loads[10].wait()
        sent(16, ssem1)


def on_device(
    krylov_block, blade_class, neighbors, iface_rows, face_rows, stiffness, lumped_mass, precond
):
    vmem = pl.BlockSpec(memory_space=pltpu.VMEM)
    hbm = pl.BlockSpec(memory_space=pltpu.HBM)
    return pl.pallas_call(
        kernel,
        out_shape=jax.ShapeDtypeStruct((1, 8, 16, 384), F32),
        in_specs=[hbm] * 9,
        out_specs=vmem,
        scratch_shapes=[
            pltpu.VMEM((2, 2, 3, 16, 256), F32),
            pltpu.SMEM((2,), jnp.int32),
            pltpu.VMEM((8, 256), jnp.int32),
            pltpu.VMEM((2, 64), jnp.int32),
            pltpu.VMEM((2, 64), jnp.int32),
            pltpu.VMEM((3, 3, 8, 256), F32),
            pltpu.VMEM((3, 256), F32),
            pltpu.VMEM((1, 8, 384, 384), BF),
            pltpu.VMEM((2, 512, 512), BF),
            pltpu.VMEM((2, 48, 128), BF),
            pltpu.VMEM((2, 48, 128), BF),
            pltpu.VMEM((2, 48, 128), BF),
            pltpu.VMEM((2, 48, 128), BF),
            pltpu.VMEM((2, 8, 24, 128), BF),
            pltpu.VMEM((32, 24, 128), BF),
            pltpu.VMEM((2, 256, 256), F32),
            pltpu.VMEM((32, 24, 128), BF),
            pltpu.VMEM((2, 8, 24, 128), BF),
            pltpu.VMEM((8, 256, 256), BF),
            pltpu.VMEM((3, 2, 16, 256), F32),
            pltpu.VMEM((8, 384, 384), BF),
            pltpu.VMEM((256, 512), BF),
            pltpu.SemaphoreType.REGULAR,
            pltpu.SemaphoreType.DMA((12,)),
            pltpu.SemaphoreType.DMA((4,)),
            pltpu.SemaphoreType.DMA((4,)),
            pltpu.SemaphoreType.DMA,
            pltpu.SemaphoreType.DMA((2,)),
            pltpu.SemaphoreType.DMA((2,)),
            pltpu.SemaphoreType.DMA((2,)),
        ],
        compiler_params=pltpu.CompilerParams(
            collective_id=0, has_side_effects=True, vmem_limit_bytes=40 * 1024 * 1024
        ),
    )(
        *(
            pltpu.with_memory_space_constraint(operand, pltpu.HBM)
            for operand in (
                krylov_block, blade_class, neighbors, iface_rows, face_rows, stiffness, lumped_mass,
                precond, jnp.asarray(kron_table()),
            )
        )
    )


def solution(mesh):
    return jax.shard_map(
        on_device,
        mesh=mesh,
        in_specs=(
            P(None, "wheel", None, None, "slab"),
            P("wheel"),
            P(None, "slab"),
            P(None, "slab"),
            P(None, "slab"),
            P(None, None, None, "slab"),
            P(None, "slab"),
            P("wheel", "slab", None, None),
        ),
        out_specs=P("wheel", "slab", None, None),
        check_vma=False,
    )
```

```python
import math

import jax
import jax.numpy as jnp
import numpy as np
from jax import lax
from jax.experimental import pallas as pl
from jax.experimental.pallas import tpu as pltpu
from jax.sharding import PartitionSpec as P

import ml_dtypes

damping_ratio = 0.5
gyro_rate = 0.8
shift_value = 0.3
class_step = 0.125

SECT = 64
WHEEL = 32
SLAB = 8
MESH = pl.DeviceIdType.MESH
BF = jnp.bfloat16
F32 = jnp.float32


def slot_of(w):
    return (w // 8 % 2) * 16 + (w // 16) * 8 + w % 8


def worker_of(t, g):
    return (g // 4) * 16 + (g % 4) * 2 + t


def basis_table():
    b = np.arange(SECT)[:, None]
    s = np.arange(SECT)[None, :]
    p, q = b // 2, b % 2
    angle = 2.0 * math.pi / SECT * ((p * s) % SECT)
    inner = np.where(q == 0, np.cos(angle), np.sin(angle)) * math.sqrt(2.0 / SECT)
    edge = np.where(q == 0, 1.0, 1.0 - 2.0 * (s % 2)) * math.sqrt(1.0 / SECT)
    return np.where(p == 0, edge, inner).astype(np.float32)


def kron_table():
    sectors = [2 * w + part for w in sorted(range(WHEEL), key=slot_of) for part in range(2)]
    full = np.kron(basis_table()[:, sectors], np.eye(8, dtype=np.float32))
    high = full.astype(ml_dtypes.bfloat16)
    low = (full - high.astype(np.float32)).astype(ml_dtypes.bfloat16)
    return np.stack((high, low))


def one_hot(rows, cols, index_row):
    at = lax.broadcasted_iota(jnp.int32, (rows, cols), 0)
    return jnp.where(at == index_row, 1.0, 0.0).astype(BF)


def kernel(
    kb_hbm, bc_hbm, nb_hbm, ifr_hbm, fcr_hbm, st_hbm, ms_hbm, pc_hbm, km_hbm, out,
    kb, bc, nb, ifr, fcr, st, ms, pcv, kmv, hs, hsw, hr, hrw, sb, rv1, acc, sb2, rv2, hot, base, flip, pick_hot,
    ready, lsem, hsend, hrecv, ssem1, rsem1, ssem2, rsem2,
):
    w = lax.axis_index("wheel")
    j = lax.axis_index("slab")

    up = lax.rem(j + 1, SLAB)
    down = lax.rem(j + SLAB - 1, SLAB)
    nxt = lax.rem(w + 1, WHEEL)
    prv = lax.rem(w + WHEEL - 1, WHEEL)
    loads = [
        pltpu.make_async_copy(src, dst, lsem.at[n])
        for n, (src, dst) in enumerate(
            (
                (ifr_hbm, ifr), (fcr_hbm, fcr),
                *((kb_hbm.at[t, p], kb.at[t, p]) for p in range(2) for t in range(2)),
                (nb_hbm, nb), (st_hbm, st), (ms_hbm, ms), (bc_hbm, bc), (km_hbm, kmv), (pc_hbm, pcv),
            )
        )
    ]
    for load in loads:
        load.start()

    barrier = pltpu.get_barrier_semaphore()
    has_up = j < SLAB - 1
    has_down = j > 0

    def greet(to):
        pl.semaphore_signal(barrier, inc=1, device_id=to, device_id_type=MESH)

    @pl.when(has_up)
    def _():
        greet({"slab": up})

    @pl.when(has_down)
    def _():
        greet({"slab": down})

    greet({"wheel": nxt})
    greet({"wheel": prv})

    my_t = lax.rem(w, 2)
    along = lax.rem(w // 2, 8)
    my_g = (w // 16) * 4 + along
    works = along < 4

    late = jnp.logical_not(works)
    side = (w < 16)
    relayed = late & side
    direct = late & jnp.logical_not(side)

    @pl.when(works)
    def _():
        mine = (w // 16) * 8 + lax.rem(w, 8)

        @pl.loop(1, 16)
        def _(i):
            other = lax.rem(mine + i, 16)
            greet({"wheel": (other // 8) * 16 + lax.rem(other, 8)})

        @pl.loop(0, 8)
        def _(i):
            greet({"wheel": 24 + i})

    @pl.when(relayed)
    def _():
        greet({"wheel": w - 2 * jnp.where(along == 7, 7, along - 3)})

    for load in loads[:2]:
        load.wait()
    none = jnp.full((1, 64), -1, jnp.int32)
    index = jnp.concatenate(
        (ifr[1:2, :], none, none, ifr[0:1, :], fcr[1:2, :], none, none, fcr[0:1, :]), axis=1
    )
    pick_hot[...] = one_hot(256, 512, index)
    for load in loads[2:6]:
        load.wait()
    u = kb[0]
    v = kb[1]
    e = (u + damping_ratio * v).reshape(96, 256)
    ehi = e.astype(BF)

    picks = jnp.dot(ehi, pick_hot[...], preferred_element_type=F32)
    hs[0] = (picks[0:48, 0:128] + pltpu.roll(picks[48:96, 0:128], 64, 1)).astype(BF)
    hs[1] = (pltpu.roll(picks[0:48, 128:256], 64, 1) + picks[48:96, 128:256]).astype(BF)
    hsw[0] = picks[48:96, 256:384].astype(BF)
    hsw[1] = picks[0:48, 384:512].astype(BF)

    told = jnp.where(along == 3, 3, 0) + jnp.where(along == 0, 1, 0)
    greeted = jnp.where(works, 15 + jnp.where(side, told, 0), jnp.where(direct, 16, 0))
    pl.semaphore_wait(
        barrier, 2 + jnp.where(has_up, 1, 0) + jnp.where(has_down, 1, 0) + greeted
    )

    def tell(to):
        pl.semaphore_signal(ready, inc=1, device_id={"wheel": to}, device_id_type=MESH)

    @pl.when(side & (along == 3))
    def _():
        for step in (2, 4, 6):
            tell(w + step)

    @pl.when(side & (along == 0))
    def _():
        tell(w + 14)

    halos = [
        pltpu.make_async_remote_copy(
            src_ref=src, dst_ref=dst, send_sem=hsend.at[n], recv_sem=hrecv.at[n],
            device_id=to, device_id_type=MESH,
        )
        for n, (src, dst, to) in enumerate(
            (
                (hs.at[0], hr.at[0], {"slab": up}),
                (hs.at[1], hr.at[1], {"slab": down}),
                (hsw.at[0], hrw.at[0], {"wheel": nxt}),
                (hsw.at[1], hrw.at[1], {"wheel": prv}),
            )
        )
    ]

    @pl.when(has_up)
    def _():
        halos[0].start()

    @pl.when(has_down)
    def _():
        halos[1].start()

    halos[2].start()
    halos[3].start()

    lane = lax.broadcasted_iota(jnp.int32, (32, 128), 1)
    spot = lane // 32

    def squeeze(a, b, c, d, spare):
        turned = [pltpu.roll(d, shift, d.ndim - 1) for shift in (96, 64, 32)]
        return jnp.concatenate(
            [jnp.where(spare, x, y) for x, y in zip(turned, (a, b, c))], axis=-2
        )

    def fourth(a, b, c, place, first):
        axis = a.ndim - 1
        return jnp.where(
            place == first,
            pltpu.roll(a, 32, axis),
            jnp.where(place == lax.rem(first + 1, 4), pltpu.roll(b, 64, axis), pltpu.roll(c, 96, axis)),
        )

    def pack(t, res):
        for h in range(2):
            part = [res[:, c, :, h * 128 : (h + 1) * 128].reshape(32, 128) for c in range(3)]
            one = pltpu.roll(part[1], 32, 1)
            two = pltpu.roll(part[2], 64, 1)
            for g in range(4):
                tile = jnp.where(
                    spot == (g + 1) % 4, one, jnp.where(spot == (g + 2) % 4, two, part[0])
                )
                sb[t, h * 4 + g] = squeeze(
                    tile[0:8], tile[16:24], tile[8:16], tile[24:32], spot[:8] == (g + 3) % 4
                ).astype(BF)

    slot = lax.rem(w // 8, 2) * 16 + (w // 16) * 8 + lax.rem(w, 8)
    half_sem = rsem1.at[lax.rem(w // 8, 2)]

    def send(t):
        for n in range(8):
            g = lax.rem(n + 4 * (1 - w // 16), 8)
            to = (g // 4) * 16 + (n % 4) * 2 + t

            @pl.when(w != to)
            def _():
                pltpu.make_async_remote_copy(
                    src_ref=sb.at[t, g], dst_ref=rv1.at[slot], send_sem=ssem1, recv_sem=half_sem,
                    device_id={"wheel": to}, device_id_type=MESH,
                ).start()

            @pl.when(w == to)
            def _():
                pltpu.make_async_copy(sb.at[t, g], rv1.at[slot], half_sem).start()

    pack(0, v - shift_value * u)

    @pl.when(works | direct)
    def _():
        send(0)

    def stencil(ke, k, picked):
        picked = picked.reshape(2, 3, 16, 256)
        for c in range(3):
            for d in range(3):
                ke[c] = ke[c] + st[c, d, k : k + 1, :] * picked[:, d]
        return ke

    for load in loads[6:10]:
        load.wait()
    elo = (e - ehi.astype(F32)).astype(BF)
    own = jnp.concatenate((ehi, elo), axis=0)
    ke = [jnp.zeros((2, 16, 256), F32) for _ in range(3)]
    for k in range(8):
        both = jnp.dot(own, one_hot(256, 256, nb[k : k + 1, :]), preferred_element_type=F32)
        ke = stencil(ke, k, both[:96] + both[96:])

    for k in range(8):
        hot[k] = one_hot(256, 256, nb[k : k + 1, :] - 256)
    mass = [ms[c : c + 1, :] for c in range(3)]
    gyro = (-(mass[0] * v[:, 1]), mass[1] * v[:, 0], None)
    scale = [1.0 + class_step * bc[s].astype(F32) for s in range(2)]

    def scaled(part):
        return jnp.stack([scale[s] * part[s] for s in range(2)], axis=0)

    for c in range(3):
        row = -scaled(ke[c]) - shift_value * (mass[c] * v[:, c])
        if c < 2:
            row = row - gyro_rate * gyro[c]
        base[c] = row

    @pl.when(relayed)
    def _():
        pl.semaphore_wait(ready, 1)
        send(0)

    @pl.when(has_up)
    def _():
        halos[0].wait_send()
        halos[1].wait_recv()

    @pl.when(jnp.logical_not(has_up))
    def _():
        hr[1] = jnp.zeros((48, 128), BF)

    @pl.when(has_down)
    def _():
        halos[1].wait_send()
        halos[0].wait_recv()

    @pl.when(jnp.logical_not(has_down))
    def _():
        hr[0] = jnp.zeros((48, 128), BF)

    halos[2].wait()
    halos[3].wait()
    lower, upper = hr[0].astype(F32), hr[1].astype(F32)
    left_half = lax.broadcasted_iota(jnp.int32, (48, 128), 1) < 64
    iface = jnp.concatenate(
        (
            jnp.where(left_half, lower, pltpu.roll(upper, 64, 1)),
            jnp.where(left_half, pltpu.roll(lower, 64, 1), upper),
        ),
        axis=0,
    )
    face = jnp.concatenate(
        (
            hrw[0].astype(F32) + picks[48:96, 384:512],
            hrw[1].astype(F32) + picks[0:48, 256:384],
        ),
        axis=0,
    )
    halo = jnp.concatenate((iface, face), axis=1).astype(BF)
    ke = [jnp.zeros((2, 16, 256), F32) for _ in range(3)]
    for k in range(8):
        ke = stencil(ke, k, jnp.dot(halo, hot[k], preferred_element_type=F32))
    rows = [base[c] - scaled(ke[c]) for c in range(3)]
    pack(1, jnp.stack(rows, axis=1))
    send(1)

    loads[11].wait()
    for g in range(8):
        turned = pcv[0, g].T
        for n, part in enumerate((0, 2, 1, 3)):
            flip[g, n * 96 : n * 96 + 96] = turned[part * 96 : part * 96 + 96]

    def sent(count, sem):
        whole = rv1.at[pl.ds(0, count)]
        pltpu.make_async_copy(whole, whole, sem).wait()

    @pl.when(works)
    def _():
        loads[10].wait()

        corner = lax.rem(my_g, 4)
        place = lax.broadcasted_iota(jnp.int32, (16, 8, 128), 2) // 32

        def field(part):
            got = rv1[part * 16 : part * 16 + 16].astype(F32)
            a, b, c = (got[:, n * 8 : n * 8 + 8] for n in range(3))
            d = fourth(a, b, c, place, corner)
            return jnp.concatenate(
                [
                    jnp.concatenate(pair, axis=1).astype(BF).reshape(256, 128)
                    for pair in ((a, b), (c, d))
                ],
                axis=1,
            )

        def transform(first, part, data):
            rows = slice(first * 256, first * 256 + 256)
            cols = slice(part * 256, part * 256 + 256)
            return jnp.dot(kmv[0, rows, cols], data, preferred_element_type=F32) + jnp.dot(
                kmv[1, rows, cols], data, preferred_element_type=F32
            )

        def arrived(part):
            whole = rv1.at[pl.ds(part * 16, 16)]
            pltpu.make_async_copy(whole, whole, rsem1.at[part]).wait()

        def answer(to, group):
            @pl.when(w != to)
            def _():
                pltpu.make_async_remote_copy(
                    src_ref=sb2.at[to], dst_ref=rv2.at[my_t, my_g], send_sem=ssem2.at[group],
                    recv_sem=rsem2.at[my_t], device_id={"wheel": to}, device_id_type=MESH,
                ).start()

            @pl.when(w == to)
            def _():
                pltpu.make_async_copy(sb2.at[to], rv2.at[my_t, my_g], rsem2.at[my_t]).start()

        arrived(0)
        near = field(0)
        for first in range(2):
            acc[first] = transform(first, 0, near)
        arrived(1)
        far = field(1)
        for first in range(2):
            har = (acc[first] + transform(first, 1, far)).reshape(16, 2, 8, 256)
            sb2[first * 16 : first * 16 + 16] = squeeze(
                har[:, 0, :, :128], har[:, 0, :, 128:], har[:, 1, :, :128], har[:, 1, :, 128:],
                place == lax.rem(corner + 3, 4),
            ).astype(BF)
            for z in (0, 1, 2, 3):
                for core in range(2):
                    answer(first * 16 + z * 2 + core, 0)

        sent(15, ssem2.at[0])
        for first in range(2):
            for z in (5, 6, 7, 4):
                for core in range(2):
                    answer(first * 16 + z * 2 + core, 1)

    lane16 = lax.broadcasted_iota(jnp.int32, (16, 128), 1)

    def placed(t, g, q, at):
        shift = (at - 32 * (g % 4)) % 128
        got = rv2[t, g].astype(F32)
        if q == 0:
            x = got[:16]
        else:
            last = fourth(got[:8], got[8:16], got[16:], lane16[:8] // 32, g % 4)
            x = jnp.concatenate((got[16:], last), axis=0)
        return pltpu.roll(x, shift, 1) if shift else x

    def product(t, g):
        top = placed(t, g, 1, 96)
        lhs = jnp.concatenate(
            (jnp.where(lane16 < 96, placed(t, g, 0, 0), top), top), axis=1
        ).astype(BF)
        return jnp.dot(
            lhs[:, :192], flip[g, t * 192 : t * 192 + 192], preferred_element_type=F32
        )

    pltpu.make_async_copy(rv2.at[0], rv2.at[0], rsem2.at[0]).wait()
    for g in range(8):
        out[0, g] = product(0, g)

    pltpu.make_async_copy(rv2.at[1], rv2.at[1], rsem2.at[1]).wait()
    for g in range(8):
        out[0, g] += product(1, g)

    @pl.when(works)
    def _():
        sent(15, ssem1)
        sent(16, ssem2.at[1])

    @pl.when(late)
    def _():
        loads[10].wait()
        sent(16, ssem1)


def on_device(
    krylov_block, blade_class, neighbors, iface_rows, face_rows, stiffness, lumped_mass, precond
):
    vmem = pl.BlockSpec(memory_space=pltpu.VMEM)
    hbm = pl.BlockSpec(memory_space=pltpu.HBM)
    return pl.pallas_call(
        kernel,
        out_shape=jax.ShapeDtypeStruct((1, 8, 16, 384), F32),
        in_specs=[hbm] * 9,
        out_specs=vmem,
        scratch_shapes=[
            pltpu.VMEM((2, 2, 3, 16, 256), F32),
            pltpu.SMEM((2,), jnp.int32),
            pltpu.VMEM((8, 256), jnp.int32),
            pltpu.VMEM((2, 64), jnp.int32),
            pltpu.VMEM((2, 64), jnp.int32),
            pltpu.VMEM((3, 3, 8, 256), F32),
            pltpu.VMEM((3, 256), F32),
            pltpu.VMEM((1, 8, 384, 384), BF),
            pltpu.VMEM((2, 512, 512), BF),
            pltpu.VMEM((2, 48, 128), BF),
            pltpu.VMEM((2, 48, 128), BF),
            pltpu.VMEM((2, 48, 128), BF),
            pltpu.VMEM((2, 48, 128), BF),
            pltpu.VMEM((2, 8, 24, 128), BF),
            pltpu.VMEM((32, 24, 128), BF),
            pltpu.VMEM((2, 256, 256), F32),
            pltpu.VMEM((32, 24, 128), BF),
            pltpu.VMEM((2, 8, 24, 128), BF),
            pltpu.VMEM((8, 256, 256), BF),
            pltpu.VMEM((3, 2, 16, 256), F32),
            pltpu.VMEM((8, 384, 384), BF),
            pltpu.VMEM((256, 512), BF),
            pltpu.SemaphoreType.REGULAR,
            pltpu.SemaphoreType.DMA((12,)),
            pltpu.SemaphoreType.DMA((4,)),
            pltpu.SemaphoreType.DMA((4,)),
            pltpu.SemaphoreType.DMA,
            pltpu.SemaphoreType.DMA((2,)),
            pltpu.SemaphoreType.DMA((2,)),
            pltpu.SemaphoreType.DMA((2,)),
        ],
        compiler_params=pltpu.CompilerParams(
            collective_id=0, has_side_effects=True, vmem_limit_bytes=40 * 1024 * 1024
        ),
    )(
        *(
            pltpu.with_memory_space_constraint(operand, pltpu.HBM)
            for operand in (
                krylov_block, blade_class, neighbors, iface_rows, face_rows, stiffness, lumped_mass,
                precond, jnp.asarray(kron_table()),
            )
        )
    )


def solution(mesh):
    return jax.shard_map(
        on_device,
        mesh=mesh,
        in_specs=(
            P(None, "wheel", None, None, "slab"),
            P("wheel"),
            P(None, "slab"),
            P(None, "slab"),
            P(None, "slab"),
            P(None, None, None, "slab"),
            P(None, "slab"),
            P("wheel", "slab", None, None),
        ),
        out_specs=P("wheel", "slab", None, None),
        check_vma=False,
    )
```
